512 devices in a mesh: db: 16 (over y_hi, x, core), pb: 32 (over y_lo, z).
Axes of the slice: x: 4, y: 4 (y_hi: 2, y_lo: 2; y = y_hi * 2 + y_lo), z: 16, core: 2. Of those that a mesh axis runs over, the one named last changes fastest.
Arguments:
- queries: bfloat16 [8192, 768], P(('db', 'pb')), may hold values from -14 to 14
- passage_codes: int32 [65536, 64], P(('db', 'pb')), may hold values from 0 to 255
- codebooks: bfloat16 [64, 12, 256], replicated, may hold values from -4 to 4
- positives: int32 [8192], P(('db', 'pb')), may hold values from 0 to 2047
- loss_weight: float32 [8192], P(('db', 'pb')), may hold values from -12 to 12
Outputs:
- query_loss: float32 [8192], P(('db', 'pb'))
- grad_queries: float32 [8192, 768], P(('db', 'pb'))
- grad_codebooks: float32 [64, 12, 256], replicated
The draws below stay inside these ranges and needn't reach their ends.
All inputs are finite; a program needn't handle non-finite values.
Results may differ from the reference program's by a relative error of at most 0.0055.
Values may be sent and summed in bfloat16 or wider, within the bound.
No kernel may reach another device: no remote copies, remote signals or barrier semaphores. Data moves between devices by JAX's collectives and lax.ppermute only.
A program may use at most 64 MiB of HBM per device.

```python
import math
import jax
import jax.numpy as jnp
from jax import lax

BOOKS = 64
SUBDIM = 12
LEVELS = 256
Q_DEV = 16
P_DEV = 128
D = 768
QUERIES = 8192
PASSAGES = 65536
GROUPS = 32
GROUP_P = 2048
N_DB = 16


def draw_queries(key, part):
    first_key = jax.random.fold_in(key, 0)
    values = jnp.clip(jax.random.normal(first_key, (QUERIES, D), jnp.float32), -6.0, 6.0)
    return values.astype(jnp.bfloat16)


def draw_codebooks(key, part):
    values = jnp.clip(jax.random.normal(key, (BOOKS, SUBDIM, LEVELS), jnp.float32), -4.0, 4.0)
    return values.astype(jnp.bfloat16)


def set_ends(result, key, low, largest):
    spot = [jax.random.randint(jax.random.fold_in(key, axis), (), 0, length) for axis, length in enumerate(result.shape)]
    widest = result.shape.index(max(result.shape))
    beside = spot[:widest] + [(spot[widest] + 1) % result.shape[widest]] + spot[widest + 1:]
    return result.at[tuple(spot)].set(low).at[tuple(beside)].set(largest)


def block_levels(rng, dims, shards, low, top_value):
    gain = 1.0
    for axis_at, blocks in shards:
        heights = jax.random.uniform(jax.random.fold_in(jax.random.fold_in(rng, 6), axis_at), (blocks,), jnp.float32, low / len(shards), top_value / len(shards))
        gain = gain * jnp.repeat(jnp.exp(heights), dims[axis_at] // blocks).reshape((-1,) + (1,) * (len(dims) - 1 - axis_at))
    return gain


def noise(key, dims, width, most, pieces=(), kind=jnp.bfloat16):
    result = jax.random.normal(key, dims, jnp.float32) * width
    if len(pieces) > 0:
        result = block_levels(key, dims, pieces, -0.22, 0.18) * result
    return jnp.clip(result, min=-most, max=most).astype(kind)


def setup_inputs(seed: int = 0) -> dict:
    arg_keys = jax.random.split(jax.random.key(seed), 6)
    queries = draw_queries(jax.random.fold_in(arg_keys[5], 71), 0)
    passage_codes = set_ends(jax.random.randint(arg_keys[1], (PASSAGES, BOOKS), 0, LEVELS), jax.random.fold_in(arg_keys[1], 1), 0, LEVELS - 1).astype(jnp.int32)
    codebooks = draw_codebooks(jax.random.fold_in(arg_keys[5], 71), 0)
    positives = set_ends(jax.random.randint(arg_keys[3], (QUERIES,), 0, GROUP_P), jax.random.fold_in(arg_keys[3], 1), 0, GROUP_P - 1).astype(jnp.int32)
    loss_weight = noise(arg_keys[4], (QUERIES,), 2.0, 12.0, ((0, 512),), jnp.float32)
    return {"queries": queries, "passage_codes": passage_codes, "codebooks": codebooks, "positives": positives, "loss_weight": loss_weight}


def decode(codebooks, passage_codes):
    passage_count, book_count = passage_codes.shape
    code_index = jnp.broadcast_to(passage_codes.T[:, None, :], (book_count, codebooks.shape[1], passage_count))
    picked = jnp.take_along_axis(codebooks, code_index, axis=2)
    return picked.transpose(2, 0, 1).reshape(passage_count, book_count * codebooks.shape[1])

def regroup(source_array, block_rows):
    trailing = source_array.shape[1:]
    reordered = source_array.reshape((N_DB, GROUPS, block_rows) + trailing)
    return jnp.swapaxes(reordered, 0, 1).reshape((GROUPS, N_DB * block_rows) + trailing)

def ungroup(grouped, block_rows):
    trailing = grouped.shape[2:]
    reordered = grouped.reshape((GROUPS, N_DB, block_rows) + trailing)
    return jnp.swapaxes(reordered, 0, 1).reshape((GROUPS * N_DB * block_rows,) + trailing)

def reference(queries, passage_codes, codebooks, positives, loss_weight):
    logit_scale = 2.5 / math.sqrt(D)
    query_sets = regroup(queries, Q_DEV)
    code_sets = regroup(passage_codes, P_DEV)
    positive_sets = regroup(positives, Q_DEV)
    weight_sets = regroup(loss_weight, Q_DEV)

    def one_group(book_total, group_items):
        query_rows, group_codes, positive_rows, weight_rows = group_items
        decoded = decode(codebooks, group_codes)
        scores = jnp.dot(query_rows, decoded.T, preferred_element_type=jnp.float32) * logit_scale
        row_max = lax.optimization_barrier(jnp.max(scores, axis=1, keepdims=True))
        log_total = row_max[:, 0] + jnp.log(lax.optimization_barrier(jnp.sum(jnp.exp(scores - row_max), axis=1)))
        is_positive = positive_rows[:, None] == jnp.arange(GROUP_P, dtype=jnp.int32)[None, :]
        chosen = lax.optimization_barrier(jnp.sum(jnp.where(is_positive, scores, 0.0), axis=1))
        group_loss = weight_rows * (log_total - chosen)
        coefficient = (weight_rows[:, None] * (jnp.exp(scores - log_total[:, None]) - is_positive.astype(jnp.float32)) * logit_scale).astype(jnp.bfloat16)
        query_grad = jnp.dot(coefficient, decoded, preferred_element_type=jnp.float32)
        passage_grad = jnp.dot(coefficient.T, query_rows, preferred_element_type=jnp.float32)
        split_grad = passage_grad.reshape(GROUP_P, BOOKS, SUBDIM)
        book_grad = jnp.zeros((BOOKS, LEVELS, SUBDIM), jnp.float32).at[jnp.arange(BOOKS)[None, :], group_codes].add(split_grad)
        return (book_total + book_grad, (group_loss, query_grad))
    start_book = jnp.zeros((BOOKS, LEVELS, SUBDIM), jnp.float32)
    book_total, (loss_sets, grad_sets) = lax.scan(one_group, start_book, (query_sets, code_sets, positive_sets, weight_sets))
    query_loss = ungroup(loss_sets, Q_DEV)
    grad_queries = ungroup(grad_sets, Q_DEV)
    return (query_loss, grad_queries, book_total.transpose(0, 2, 1))
```

```python
import functools
import math

import jax
import jax.numpy as jnp
from jax import lax
from jax.experimental import pallas as pl
from jax.experimental.pallas import tpu as pltpu
from jax.sharding import PartitionSpec as P

LANES = 128


def pack_kernel(queries_ref, codes_ref, weight_ref, positive_ref, out_ref):
    rows, width = queries_ref.shape
    books = codes_ref.shape[1]
    for j in range(width // LANES):
        out_ref[rows * j : rows * (j + 1), :] = queries_ref[:, LANES * j : LANES * (j + 1)]
    top = rows * (width // LANES)
    code_rows = codes_ref[...].astype(jnp.float32).T
    out_ref[top : top + books, :] = code_rows.astype(jnp.bfloat16)
    spot = lax.broadcasted_iota(jnp.int32, (rows, rows), 0)
    lane = lax.broadcasted_iota(jnp.int32, (rows, rows), 1)

    def column(row):
        spread = jnp.broadcast_to(row, (rows, rows))
        return jnp.sum(jnp.where(spot == lane, spread, 0.0), axis=1, keepdims=True)

    weight = column(weight_ref[...])
    positive = positive_ref[...]
    first = weight.astype(jnp.bfloat16).astype(jnp.float32)
    second = (weight - first).astype(jnp.bfloat16).astype(jnp.float32)
    third = weight - first - second
    block = column((positive // LANES).astype(jnp.float32))
    place = column((positive % LANES).astype(jnp.float32))
    wide = lax.broadcasted_iota(jnp.int32, (rows, LANES), 1)
    extra = jnp.zeros((rows, LANES), jnp.float32)
    for j, value in enumerate((first, second, third, block, place)):
        extra = jnp.where(wide == j, value, extra)
    out_ref[top + books :, :] = extra.astype(jnp.bfloat16)


def main_kernel(
    scale, me_ref, group_ref, cb_ref, codes_ref,
    loss_ref, gq_ref, gb_ref,
    code_scr, cb_scr, q_scr, dec_scr, s_scr, total_scr,
):
    members, _, _ = group_ref.shape
    width = cb_ref.shape[0]
    books = codes_ref.shape[1]
    rows = gq_ref.shape[0]
    blocks = width // LANES
    top = rows * blocks
    queries = members * rows
    me = me_ref[0, 0]
    code_scr[...] = group_ref[:, top : top + books, :].astype(jnp.float32).astype(jnp.int32)
    cb_scr[...] = cb_ref[...].astype(jnp.float32)
    for j in range(blocks):
        q_scr[:, LANES * j : LANES * (j + 1)] = group_ref[
            :, rows * j : rows * (j + 1), :
        ].reshape(queries, LANES)
    low_rows = lax.broadcasted_iota(jnp.int32, (8, LANES), 0) < 4

    def decode_block(d, carry):
        for four in range(books // 4):
            tiles = []
            for pair in (2 * four, 2 * four + 1):
                first = jnp.broadcast_to(code_scr[d, 2 * pair : 2 * pair + 1, :], (8, LANES))
                second = jnp.broadcast_to(
                    code_scr[d, 2 * pair + 1 : 2 * pair + 2, :], (8, LANES)
                )
                for t, index in enumerate((first, jnp.where(low_rows, first, second), second)):
                    at = 24 * pair + 8 * t
                    inner = index & (LANES - 1)
                    low = jnp.take_along_axis(cb_scr[at : at + 8, :LANES], inner, axis=1)
                    high = jnp.take_along_axis(cb_scr[at : at + 8, LANES:], inner, axis=1)
                    tiles.append(jnp.where(index >= LANES, high, low))
            dec_scr[d, 48 * four : 48 * four + 48, :] = jnp.concatenate(tiles, axis=0).astype(
                jnp.bfloat16
            )
        s_scr[d] = (
            jnp.dot(q_scr[...], dec_scr[d], preferred_element_type=jnp.float32) * scale
        )
        return carry

    lax.fori_loop(0, members, decode_block, 0)

    highest = s_scr[0]
    for d in range(1, members):
        highest = jnp.maximum(highest, s_scr[d])
    row_max = jnp.max(highest, axis=1, keepdims=True)
    total = jnp.exp(s_scr[0] - row_max)
    for d in range(1, members):
        total = total + jnp.exp(s_scr[d] - row_max)
    log_total = row_max + jnp.log(jnp.sum(total, axis=1, keepdims=True))
    total_scr[...] = jnp.broadcast_to(log_total, (queries, LANES))

    def extras(block):
        weight = block[:, 0:1] + block[:, 1:2] + block[:, 2:3]
        return weight, block[:, 3:4], block[:, 4:5]

    extra = group_ref[:, top + books :, :].reshape(queries, LANES).astype(jnp.float32)
    weight, block, place = extras(extra)
    here = me.astype(jnp.float32)
    lane = lax.broadcasted_iota(jnp.int32, (queries, LANES), 1).astype(jnp.float32)
    is_positive = jnp.where((block == here) & (place == lane), 1.0, 0.0)
    coefficient = (
        weight * (jnp.exp(s_scr[me] - total_scr[...]) - is_positive) * scale
    ).astype(jnp.bfloat16)
    passage_grad = lax.dot_general(
        q_scr[...], coefficient, (((0,), (0,)), ((), ())), preferred_element_type=jnp.float32
    )

    own = pl.ds(pl.multiple_of(me * rows, rows), rows)
    weight, block, place = extras(group_ref[me, top + books :, :].astype(jnp.float32))
    own_total = total_scr[own, :]
    own_lane = lax.broadcasted_iota(jnp.int32, (rows, LANES), 1).astype(jnp.float32)
    chosen = jnp.zeros((rows, LANES), jnp.float32)
    grad = jnp.zeros((rows, width), jnp.float32)
    for d in range(members):
        scores = s_scr[d, own, :]
        hit = (block == float(d)) & (place == own_lane)
        chosen = chosen + jnp.where(hit, scores, 0.0)
        part = (
            weight * (jnp.exp(scores - own_total) - jnp.where(hit, 1.0, 0.0)) * scale
        ).astype(jnp.bfloat16)
        grad = grad + lax.dot_general(
            part, dec_scr[d], (((1,), (1,)), ((), ())), preferred_element_type=jnp.float32
        )
    gq_ref[...] = grad
    loss = weight * (own_total - jnp.sum(chosen, axis=1, keepdims=True))
    diagonal = lax.broadcasted_iota(jnp.int32, (rows, LANES), 0).astype(jnp.float32) == own_lane
    loss_ref[...] = jnp.sum(jnp.where(diagonal, loss, 0.0), axis=0, keepdims=True)[:, :rows]

    levels = cb_ref.shape[1]
    level = lax.broadcasted_iota(jnp.int32, (LANES, levels), 1)
    upper = lax.broadcasted_iota(jnp.int32, (24, LANES), 0) < 12
    for pair in range(books // 2):
        tables = [
            jnp.where(codes_ref[:, m : m + 1] == level, 1.0, 0.0).astype(jnp.bfloat16)
            for m in (2 * pair, 2 * pair + 1)
        ]
        terms = passage_grad[24 * pair : 24 * pair + 24, :]
        high = terms.astype(jnp.bfloat16).astype(jnp.float32)
        low = terms - high
        spread = [
            jnp.concatenate([jnp.where(upper, x, 0.0), jnp.where(upper, 0.0, x)], axis=1)
            for x in (high, low)
        ]
        sums = jnp.dot(
            jnp.concatenate(spread, axis=0).astype(jnp.bfloat16),
            jnp.concatenate(tables, axis=0),
            preferred_element_type=jnp.float32,
        )
        gb_ref[24 * pair : 24 * pair + 24, :] = sums[:24] + sums[24:]


def per_device(queries, passage_codes, codebooks, positives, loss_weight):
    rows, width = queries.shape
    passages, books = passage_codes.shape
    sub_width, levels = codebooks.shape[1:]
    members = lax.axis_size("db")
    others = lax.axis_size("pb")
    pack_rows = rows * (width // LANES) + books + rows
    scale = 2.5 / math.sqrt(width)
    pack = pl.pallas_call(
        pack_kernel,
        out_shape=jax.ShapeDtypeStruct((pack_rows, LANES), jnp.bfloat16),
        name="pack",
    )(queries, passage_codes, loss_weight.reshape(1, rows), positives.reshape(1, rows))
    group = lax.all_gather(pack, "db", axis=0)
    me = lax.axis_index("db").astype(jnp.int32).reshape(1, 1)
    loss, grad_queries, book_part = pl.pallas_call(
        functools.partial(main_kernel, scale),
        out_shape=(
            jax.ShapeDtypeStruct((1, rows), jnp.float32),
            jax.ShapeDtypeStruct((rows, width), jnp.float32),
            jax.ShapeDtypeStruct((width, levels), jnp.float32),
        ),
        in_specs=[pl.BlockSpec(memory_space=pltpu.SMEM)]
        + [pl.BlockSpec(memory_space=pltpu.VMEM)] * 3,
        scratch_shapes=[
            pltpu.VMEM((members, books, LANES), jnp.int32),
            pltpu.VMEM((width, levels), jnp.float32),
            pltpu.VMEM((members * rows, width), jnp.bfloat16),
            pltpu.VMEM((members, width, LANES), jnp.bfloat16),
            pltpu.VMEM((members, members * rows, LANES), jnp.float32),
            pltpu.VMEM((members * rows, LANES), jnp.float32),
        ],
        name="core",
    )(me, group, codebooks.reshape(width, levels), passage_codes)
    part = lax.all_to_all(book_part.reshape(members, -1, levels), "db", 0, 0)
    part = jnp.sum(part, axis=0)
    part = lax.all_to_all(part.reshape(others, -1), "pb", 0, 0)
    part = jnp.sum(part, axis=0)
    part = lax.all_gather(part, "pb", axis=0)
    part = lax.all_gather(part.reshape(-1, levels), "db", axis=0)
    return loss.reshape(rows), grad_queries, part.reshape(books, sub_width, levels)


def solution(mesh):
    return jax.shard_map(
        per_device,
        mesh=mesh,
        in_specs=(
            P(("db", "pb"), None),
            P(("db", "pb"), None),
            P(),
            P(("db", "pb")),
            P(("db", "pb")),
        ),
        out_specs=(P(("db", "pb")), P(("db", "pb"), None), P()),
        check_vma=False,
    )
```

```python
import functools
import math

import jax
import jax.numpy as jnp
from jax import lax
from jax.experimental import pallas as pl
from jax.experimental.pallas import tpu as pltpu
from jax.sharding import PartitionSpec as P

LANES = 128


def pack_kernel(queries_ref, codes_ref, weight_ref, positive_ref, out_ref):
    rows, width = queries_ref.shape
    books = codes_ref.shape[1]
    for j in range(width // LANES):
        out_ref[rows * j : rows * (j + 1), :] = queries_ref[:, LANES * j : LANES * (j + 1)]
    top = rows * (width // LANES)
    code_rows = codes_ref[...].astype(jnp.float32).T
    out_ref[top : top + books, :] = code_rows.astype(jnp.bfloat16)
    spot = lax.broadcasted_iota(jnp.int32, (rows, rows), 0)
    lane = lax.broadcasted_iota(jnp.int32, (rows, rows), 1)

    def column(row):
        spread = jnp.broadcast_to(row, (rows, rows))
        return jnp.sum(jnp.where(spot == lane, spread, 0.0), axis=1, keepdims=True)

    weight = column(weight_ref[...])
    positive = positive_ref[...]
    first = weight.astype(jnp.bfloat16).astype(jnp.float32)
    second = (weight - first).astype(jnp.bfloat16).astype(jnp.float32)
    third = weight - first - second
    block = column((positive // LANES).astype(jnp.float32))
    place = column((positive % LANES).astype(jnp.float32))
    wide = lax.broadcasted_iota(jnp.int32, (rows, LANES), 1)
    extra = jnp.zeros((rows, LANES), jnp.float32)
    for j, value in enumerate((first, second, third, block, place)):
        extra = jnp.where(wide == j, value, extra)
    out_ref[top + books :, :] = extra.astype(jnp.bfloat16)


def main_kernel(
    scale, me_ref, group_ref, cb_ref, codes_ref,
    loss_ref, gq_ref, gb_ref,
    code_scr, cb_scr, q_scr, dec_scr, s_scr, total_scr,
):
    members, _, _ = group_ref.shape
    width = cb_ref.shape[0]
    books = codes_ref.shape[1]
    rows = gq_ref.shape[0]
    blocks = width // LANES
    top = rows * blocks
    queries = members * rows
    me = me_ref[0, 0]
    code_scr[...] = group_ref[:, top : top + books, :].astype(jnp.float32).astype(jnp.int32)
    cb_scr[...] = cb_ref[...].astype(jnp.float32)
    for j in range(blocks):
        q_scr[:, LANES * j : LANES * (j + 1)] = group_ref[
            :, rows * j : rows * (j + 1), :
        ].reshape(queries, LANES)
    low_rows = lax.broadcasted_iota(jnp.int32, (8, LANES), 0) < 4

    def decode_block(d, carry):
        for four in range(books // 4):
            tiles = []
            for pair in (2 * four, 2 * four + 1):
                first = jnp.broadcast_to(code_scr[d, 2 * pair : 2 * pair + 1, :], (8, LANES))
                second = jnp.broadcast_to(
                    code_scr[d, 2 * pair + 1 : 2 * pair + 2, :], (8, LANES)
                )
                for t, index in enumerate((first, jnp.where(low_rows, first, second), second)):
                    at = 24 * pair + 8 * t
                    inner = index & (LANES - 1)
                    low = jnp.take_along_axis(cb_scr[at : at + 8, :LANES], inner, axis=1)
                    high = jnp.take_along_axis(cb_scr[at : at + 8, LANES:], inner, axis=1)
                    tiles.append(jnp.where(index >= LANES, high, low))
            dec_scr[d, 48 * four : 48 * four + 48, :] = jnp.concatenate(tiles, axis=0).astype(
                jnp.bfloat16
            )
        s_scr[d] = (
            jnp.dot(q_scr[...], dec_scr[d], preferred_element_type=jnp.float32) * scale
        )
        return carry

    lax.fori_loop(0, members, decode_block, 0)

    highest = s_scr[0]
    for d in range(1, members):
        highest = jnp.maximum(highest, s_scr[d])
    row_max = jnp.max(highest, axis=1, keepdims=True)
    total = jnp.exp(s_scr[0] - row_max)
    for d in range(1, members):
        total = total + jnp.exp(s_scr[d] - row_max)
    log_total = row_max + jnp.log(jnp.sum(total, axis=1, keepdims=True))
    total_scr[...] = jnp.broadcast_to(log_total, (queries, LANES))

    def extras(block):
        weight = block[:, 0:1] + block[:, 1:2] + block[:, 2:3]
        return weight, block[:, 3:4], block[:, 4:5]

    extra = group_ref[:, top + books :, :].reshape(queries, LANES).astype(jnp.float32)
    weight, block, place = extras(extra)
    here = me.astype(jnp.float32)
    lane = lax.broadcasted_iota(jnp.int32, (queries, LANES), 1).astype(jnp.float32)
    is_positive = jnp.where((block == here) & (place == lane), 1.0, 0.0)
    coefficient = (
        weight * (jnp.exp(s_scr[me] - total_scr[...]) - is_positive) * scale
    ).astype(jnp.bfloat16)
    passage_grad = lax.dot_general(
        q_scr[...], coefficient, (((0,), (0,)), ((), ())), preferred_element_type=jnp.float32
    )

    own = pl.ds(pl.multiple_of(me * rows, rows), rows)
    weight, block, place = extras(group_ref[me, top + books :, :].astype(jnp.float32))
    own_total = total_scr[own, :]
    own_lane = lax.broadcasted_iota(jnp.int32, (rows, LANES), 1).astype(jnp.float32)
    chosen = jnp.zeros((rows, LANES), jnp.float32)
    grad = jnp.zeros((rows, width), jnp.float32)
    for d in range(members):
        scores = s_scr[d, own, :]
        hit = (block == float(d)) & (place == own_lane)
        chosen = chosen + jnp.where(hit, scores, 0.0)
        part = (
            weight * (jnp.exp(scores - own_total) - jnp.where(hit, 1.0, 0.0)) * scale
        ).astype(jnp.bfloat16)
        grad = grad + lax.dot_general(
            part, dec_scr[d], (((1,), (1,)), ((), ())), preferred_element_type=jnp.float32
        )
    gq_ref[...] = grad
    loss = weight * (own_total - jnp.sum(chosen, axis=1, keepdims=True))
    diagonal = lax.broadcasted_iota(jnp.int32, (rows, LANES), 0).astype(jnp.float32) == own_lane
    loss_ref[...] = jnp.sum(jnp.where(diagonal, loss, 0.0), axis=0, keepdims=True)[:, :rows]

    levels = cb_ref.shape[1]
    level = lax.broadcasted_iota(jnp.int32, (LANES, levels), 1)
    upper = lax.broadcasted_iota(jnp.int32, (24, LANES), 0) < 12
    ready = []
    for pair in range(books // 2):
        tables = [
            jnp.where(codes_ref[:, m : m + 1] == level, 1.0, 0.0).astype(jnp.bfloat16)
            for m in (2 * pair, 2 * pair + 1)
        ]
        terms = passage_grad[24 * pair : 24 * pair + 24, :]
        high = terms.astype(jnp.bfloat16).astype(jnp.float32)
        low = terms - high
        spread = [
            jnp.concatenate([jnp.where(upper, x, 0.0), jnp.where(upper, 0.0, x)], axis=1)
            for x in (high, low)
        ]
        sums = jnp.dot(
            jnp.concatenate(spread, axis=0).astype(jnp.bfloat16),
            jnp.concatenate(tables, axis=0),
            preferred_element_type=jnp.float32,
        )
        ready.append(sums[:24] + sums[24:])
        if pair % 2 == 1:
            gb_ref[24 * pair - 24 : 24 * pair + 24, :] = jnp.concatenate(ready, axis=0).astype(
                jnp.bfloat16
            )
            ready = []


def spread(block, axis):
    copies = jnp.broadcast_to(block[None], (lax.axis_size(axis),) + block.shape)
    return lax.all_to_all(copies, axis, 0, 0)


def per_device(queries, passage_codes, codebooks, positives, loss_weight):
    rows, width = queries.shape
    passages, books = passage_codes.shape
    sub_width, levels = codebooks.shape[1:]
    members = lax.axis_size("db")
    others = lax.axis_size("pb")
    pack_rows = rows * (width // LANES) + books + rows
    scale = 2.5 / math.sqrt(width)
    pack = pl.pallas_call(
        pack_kernel,
        out_shape=jax.ShapeDtypeStruct((pack_rows, LANES), jnp.bfloat16),
        name="pack",
    )(queries, passage_codes, loss_weight.reshape(1, rows), positives.reshape(1, rows))
    group = spread(pack, "db")
    me = lax.axis_index("db").astype(jnp.int32).reshape(1, 1)
    loss, grad_queries, book_part = pl.pallas_call(
        functools.partial(main_kernel, scale),
        out_shape=(
            jax.ShapeDtypeStruct((1, rows), jnp.float32),
            jax.ShapeDtypeStruct((rows, width), jnp.float32),
            jax.ShapeDtypeStruct((width, levels), jnp.bfloat16),
        ),
        in_specs=[pl.BlockSpec(memory_space=pltpu.SMEM)]
        + [pl.BlockSpec(memory_space=pltpu.VMEM)] * 3,
        scratch_shapes=[
            pltpu.VMEM((members, books, LANES), jnp.int32),
            pltpu.VMEM((width, levels), jnp.float32),
            pltpu.VMEM((members * rows, width), jnp.bfloat16),
            pltpu.VMEM((members, width, LANES), jnp.bfloat16),
            pltpu.VMEM((members, members * rows, LANES), jnp.float32),
            pltpu.VMEM((members * rows, LANES), jnp.float32),
        ],
        name="core",
    )(me, group, codebooks.reshape(width, levels), passage_codes)
    part = lax.all_to_all(book_part.reshape(members, -1, levels), "db", 0, 0)
    part = jnp.sum(part.astype(jnp.float32), axis=0)
    part = lax.all_to_all(part.reshape(others, -1), "pb", 0, 0)
    part = jnp.sum(part, axis=0)
    part = spread(part, "pb").reshape(-1, levels).astype(jnp.bfloat16)
    part = spread(part, "db").astype(jnp.float32)
    return loss.reshape(rows), grad_queries, part.reshape(books, sub_width, levels)


def solution(mesh):
    return jax.shard_map(
        per_device,
        mesh=mesh,
        in_specs=(
            P(("db", "pb"), None),
            P(("db", "pb"), None),
            P(),
            P(("db", "pb")),
            P(("db", "pb")),
        ),
        out_specs=(P(("db", "pb")), P(("db", "pb"), None), P()),
        check_vma=False,
    )
```

```python
import functools
import math

import jax
import jax.numpy as jnp
from jax import lax
from jax.experimental import pallas as pl
from jax.experimental.pallas import tpu as pltpu
from jax.sharding import Mesh
from jax.sharding import PartitionSpec as P

LANES = 128
PLANE = ("db", "near")
WHOLE = ("db", "near", "ring")


def order_table(width, books, inverse):
    sub_width = width // books
    row = lax.broadcasted_iota(jnp.int32, (width, width), 0)
    column = lax.broadcasted_iota(jnp.int32, (1, width), 1)
    if inverse:
        source = (column % sub_width) * books + column // sub_width
    else:
        source = (column % books) * sub_width + column // books
    return jnp.where(row == source, 1.0, 0.0).astype(jnp.bfloat16)


def pack_kernel(queries_ref, codes_ref, weight_ref, positive_ref, out_ref):
    rows, width = queries_ref.shape
    books = codes_ref.shape[0]
    top = rows * (width // LANES)
    sorted_rows = jnp.dot(
        queries_ref[...], order_table(width, books, False), preferred_element_type=jnp.float32
    ).astype(jnp.bfloat16)
    code_rows = codes_ref[...].astype(jnp.float32).astype(jnp.bfloat16)
    spot = lax.broadcasted_iota(jnp.int32, (rows, rows), 0)
    lane = lax.broadcasted_iota(jnp.int32, (rows, rows), 1)

    def column(row):
        spread_row = jnp.broadcast_to(row, (rows, rows))
        return jnp.sum(jnp.where(spot == lane, spread_row, 0.0), axis=1, keepdims=True)

    weight = column(weight_ref[...])
    positive = positive_ref[...]
    first = weight.astype(jnp.bfloat16).astype(jnp.float32)
    second = (weight - first).astype(jnp.bfloat16).astype(jnp.float32)
    third = weight - first - second
    block = column((positive // LANES).astype(jnp.float32))
    place = column((positive % LANES).astype(jnp.float32))
    wide = lax.broadcasted_iota(jnp.int32, (rows, LANES), 1)
    extra = jnp.zeros((rows, LANES), jnp.float32)
    for j, value in enumerate((first, second, third, block, place)):
        extra = jnp.where(wide == j, value, extra)
    extra = extra.astype(jnp.bfloat16)
    for d in range(out_ref.shape[0]):
        for j in range(width // LANES):
            out_ref[d, rows * j : rows * (j + 1), :] = sorted_rows[:, LANES * j : LANES * (j + 1)]
        out_ref[d, top : top + books, :] = code_rows
        out_ref[d, top + books :, :] = extra


def main_kernel(
    scale, books, me_ref, group_ref, cb_ref,
    loss_ref, gq_ref, gb_ref,
    cb_scr, q_scr, dec_scr, s_scr, max_scr, sum_scr, total_scr, pg_scr, gb_scr,
):
    members = group_ref.shape[0]
    width, levels = cb_ref.shape
    sub_width = width // books
    rows = gq_ref.shape[0]
    blocks = width // LANES
    top = rows * blocks
    queries = members * rows
    me = me_ref[0, 0]
    cb_scr[...] = cb_ref[...].astype(jnp.float32)
    for j in range(blocks):
        q_scr[:, LANES * j : LANES * (j + 1)] = group_ref[
            :, rows * j : rows * (j + 1), :
        ].reshape(queries, LANES)

    def decode(t):
        for side in range(2):
            codes = (
                group_ref[2 * t + side, top : top + books, :]
                .astype(jnp.float32)
                .astype(jnp.int32)
            )
            for two in range(books // 16):
                index = [codes[16 * two + 8 * h : 16 * two + 8 * h + 8, :] for h in range(2)]
                inner = [x & (LANES - 1) for x in index]
                upper = [x >= LANES for x in index]
                for c in range(sub_width):
                    tiles = []
                    for h in range(2):
                        at = c * books + 16 * two + 8 * h
                        low = jnp.take_along_axis(cb_scr[at : at + 8, :LANES], inner[h], axis=1)
                        high = jnp.take_along_axis(cb_scr[at : at + 8, LANES:], inner[h], axis=1)
                        tiles.append(jnp.where(upper[h], high, low))
                    at = c * books + 16 * two
                    dec_scr[t, at : at + 16, LANES * side : LANES * side + LANES] = (
                        jnp.concatenate(tiles, axis=0).astype(jnp.bfloat16)
                    )

    def score(t):
        both = jnp.dot(q_scr[...], dec_scr[t], preferred_element_type=jnp.float32) * scale
        left, right = both[:, :LANES], both[:, LANES:]
        s_scr[2 * t] = left
        s_scr[2 * t + 1] = right
        newest = jnp.maximum(left, right)
        if t > 0:
            before = max_scr[...]
            newest = jnp.maximum(newest, before)
        total = jnp.exp(left - newest) + jnp.exp(right - newest)
        if t > 0:
            total = total + sum_scr[...] * jnp.exp(before - newest)
        max_scr[...] = newest
        sum_scr[...] = total

    for t in range(members // 2):
        decode(t)
        score(t)

    highest = max_scr[...]
    row_max = jnp.max(highest, axis=1, keepdims=True)
    total = jnp.sum(sum_scr[...] * jnp.exp(highest - row_max), axis=1, keepdims=True)
    total_scr[...] = jnp.broadcast_to(row_max + jnp.log(total), (queries, LANES))

    def extras(block):
        weight = block[:, 0:1] + block[:, 1:2] + block[:, 2:3]
        return weight, block[:, 3:4], block[:, 4:5]

    extra = group_ref[:, top + books :, :].reshape(queries, LANES).astype(jnp.float32)
    weight, block, place = extras(extra)
    here = me.astype(jnp.float32)
    lane = lax.broadcasted_iota(jnp.int32, (queries, LANES), 1).astype(jnp.float32)
    is_positive = jnp.where((block == here) & (place == lane), 1.0, 0.0)
    coefficient = (
        weight * (jnp.exp(s_scr[me] - total_scr[...]) - is_positive) * scale
    ).astype(jnp.bfloat16)
    pg_scr[:width, :] = lax.dot_general(
        q_scr[...], coefficient, (((0,), (0,)), ((), ())), preferred_element_type=jnp.float32
    )
    pg_scr[width:, :] = jnp.zeros((pg_scr.shape[0] - width, LANES), jnp.float32)

    own_codes = group_ref[me, top : top + books, :].astype(jnp.float32).astype(jnp.int32)
    level = lax.broadcasted_iota(jnp.int32, (levels, LANES), 0)
    nothing = jnp.zeros((16, LANES), jnp.float32)
    for m in range(0, books, 2):
        tables = [
            jnp.where(
                jnp.broadcast_to(own_codes[m + h : m + h + 1, :], (levels, LANES)) == level,
                1.0,
                0.0,
            ).astype(jnp.bfloat16)
            for h in range(2)
        ]
        parts = []
        for h in range(2):
            terms = pg_scr[pl.ds(m + h, 16, stride=books), :]
            high = terms.astype(jnp.bfloat16).astype(jnp.float32)
            for x in (high, terms - high):
                parts.append(
                    jnp.concatenate([x, nothing] if h == 0 else [nothing, x], axis=1)
                )
        sums = lax.dot_general(
            jnp.concatenate(parts, axis=0).astype(jnp.bfloat16),
            jnp.concatenate(tables, axis=1),
            (((1,), (1,)), ((), ())),
            preferred_element_type=jnp.float32,
        )
        for h in range(2):
            both = sums[32 * h : 32 * h + 16] + sums[32 * h + 16 : 32 * h + 32]
            for j in range(levels // LANES):
                gb_scr[j, pl.ds(m + h, 16, stride=books), :] = both[:, LANES * j : LANES * j + LANES]
    for j in range(levels // LANES):
        gb_ref[:, LANES * j : LANES * j + LANES] = gb_scr[j, :width, :].astype(jnp.bfloat16)

    own = pl.ds(pl.multiple_of(me * rows, rows), rows)
    weight, block, place = extras(group_ref[me, top + books :, :].astype(jnp.float32))
    own_total = total_scr[own, :]
    own_lane = lax.broadcasted_iota(jnp.int32, (rows, LANES), 1).astype(jnp.float32)
    chosen = jnp.zeros((rows, LANES), jnp.float32)
    grad = jnp.zeros((rows, width), jnp.float32)
    for t in range(members // 2):
        parts = []
        for d in (2 * t, 2 * t + 1):
            scores = s_scr[d, own, :]
            hit = (block == float(d)) & (place == own_lane)
            chosen = chosen + jnp.where(hit, scores, 0.0)
            parts.append(
                weight * (jnp.exp(scores - own_total) - jnp.where(hit, 1.0, 0.0)) * scale
            )
        grad = grad + lax.dot_general(
            jnp.concatenate(parts, axis=1).astype(jnp.bfloat16),
            dec_scr[t],
            (((1,), (1,)), ((), ())),
            preferred_element_type=jnp.float32,
        )
    first = grad.astype(jnp.bfloat16).astype(jnp.float32)
    second = (grad - first).astype(jnp.bfloat16).astype(jnp.float32)
    third = grad - first - second
    restored = jnp.dot(
        jnp.concatenate([first, second, third], axis=0).astype(jnp.bfloat16),
        order_table(width, books, True),
        preferred_element_type=jnp.float32,
    )
    gq_ref[...] = restored[:rows] + restored[rows : 2 * rows] + restored[2 * rows :]
    loss = weight * (own_total - jnp.sum(chosen, axis=1, keepdims=True))
    diagonal = lax.broadcasted_iota(jnp.int32, (rows, LANES), 0).astype(jnp.float32) == own_lane
    loss_ref[...] = jnp.sum(jnp.where(diagonal, loss, 0.0), axis=0, keepdims=True)[:, :rows]


def spread(block, axis):
    copies = jnp.broadcast_to(block[None], (lax.axis_size(axis),) + block.shape)
    return lax.all_to_all(copies, axis, 0, 0)


def per_device(queries, passage_codes, codebooks, positives, loss_weight):
    rows, width = queries.shape
    books = passage_codes.shape[1]
    sub_width, levels = codebooks.shape[1:]
    members = lax.axis_size("db")
    plane = lax.axis_size(PLANE)
    pack_rows = rows * (width // LANES) + books + rows
    scale = 2.5 / math.sqrt(width)
    pack = pl.pallas_call(
        pack_kernel,
        out_shape=jax.ShapeDtypeStruct((members, pack_rows, LANES), jnp.bfloat16),
        name="pack",
    )(queries, passage_codes.T, loss_weight.reshape(1, rows), positives.reshape(1, rows))
    group = lax.all_to_all(pack, "db", 0, 0)
    me = lax.axis_index("db").astype(jnp.int32).reshape(1, 1)
    loss, grad_queries, book_part = pl.pallas_call(
        functools.partial(main_kernel, scale, books),
        out_shape=(
            jax.ShapeDtypeStruct((1, rows), jnp.float32),
            jax.ShapeDtypeStruct((rows, width), jnp.float32),
            jax.ShapeDtypeStruct((width, levels), jnp.bfloat16),
        ),
        in_specs=[pl.BlockSpec(memory_space=pltpu.SMEM)]
        + [pl.BlockSpec(memory_space=pltpu.VMEM)] * 2,
        scratch_shapes=[
            pltpu.VMEM((width, levels), jnp.float32),
            pltpu.VMEM((members * rows, width), jnp.bfloat16),
            pltpu.VMEM((members // 2, width, 2 * LANES), jnp.bfloat16),
            pltpu.VMEM((members, members * rows, LANES), jnp.float32),
            pltpu.VMEM((members * rows, LANES), jnp.float32),
            pltpu.VMEM((members * rows, LANES), jnp.float32),
            pltpu.VMEM((members * rows, LANES), jnp.float32),
            pltpu.VMEM((16 * books, LANES), jnp.float32),
            pltpu.VMEM((levels // LANES, 16 * books, LANES), jnp.float32),
        ],
        name="core",
    )(me, group, codebooks.transpose(1, 0, 2).reshape(width, levels))
    part = lax.all_to_all(book_part.reshape(plane, -1, levels), PLANE, 0, 0)
    part = jnp.sum(part.astype(jnp.float32), axis=0).astype(jnp.bfloat16)
    part = spread(part, "ring")
    part = jnp.sum(part.astype(jnp.float32), axis=0).astype(jnp.bfloat16)
    part = spread(part, PLANE).astype(jnp.float32)
    book_total = part.reshape(sub_width, books, levels).transpose(1, 0, 2)
    return loss.reshape(rows), grad_queries, book_total


def solution(mesh):
    lines, stacks = mesh.devices.shape
    fine = Mesh(mesh.devices.reshape(lines, 2, stacks // 2), WHOLE)
    return jax.shard_map(
        per_device,
        mesh=fine,
        in_specs=(P(WHOLE, None), P(WHOLE, None), P(), P(WHOLE), P(WHOLE)),
        out_specs=(P(WHOLE), P(WHOLE, None), P()),
        check_vma=False,
    )
```

```python
import functools
import math

import jax
import jax.numpy as jnp
from jax import lax
from jax.experimental import pallas as pl
from jax.experimental.pallas import tpu as pltpu
from jax.sharding import Mesh
from jax.sharding import PartitionSpec as P

LANES = 128
PLANE = ("db", "near", "pair")
WHOLE = ("db", "near", "far", "pair")


def order_table(width, books, inverse):
    sub_width = width // books
    row = lax.broadcasted_iota(jnp.int32, (width, 1 if inverse else width), 0)
    column = lax.broadcasted_iota(jnp.int32, (width if inverse else 1, width), 1)
    place = row if inverse else column
    inner = place % (8 * sub_width)
    source = (place // (8 * sub_width) * 8 + inner % 8) * sub_width + inner // 8
    other = column if inverse else row
    return jnp.where(other == source, 1.0, 0.0).astype(jnp.bfloat16)


def pack_kernel(queries_ref, codes_ref, weight_ref, positive_ref, out_ref):
    rows, width = queries_ref.shape
    books = codes_ref.shape[0]
    top = rows * (width // LANES)
    code_rows = codes_ref[...].astype(jnp.float32).astype(jnp.bfloat16)
    spot = lax.broadcasted_iota(jnp.int32, (rows, rows), 0)
    lane = lax.broadcasted_iota(jnp.int32, (rows, rows), 1)

    def column(row):
        spread_row = jnp.broadcast_to(row, (rows, rows))
        return jnp.sum(jnp.where(spot == lane, spread_row, 0.0), axis=1, keepdims=True)

    weight = column(weight_ref[...])
    positive = positive_ref[...]
    first = weight.astype(jnp.bfloat16).astype(jnp.float32)
    second = (weight - first).astype(jnp.bfloat16).astype(jnp.float32)
    third = weight - first - second
    block = column((positive // LANES).astype(jnp.float32))
    place = column((positive % LANES).astype(jnp.float32))
    wide = lax.broadcasted_iota(jnp.int32, (rows, LANES), 1)
    extra = jnp.zeros((rows, LANES), jnp.float32)
    for j, value in enumerate((first, second, third, block, place)):
        extra = jnp.where(wide == j, value, extra)
    extra = extra.astype(jnp.bfloat16)
    for d in range(out_ref.shape[0]):
        for j in range(width // LANES):
            out_ref[d, rows * j : rows * (j + 1), :] = queries_ref[
                :, LANES * j : LANES * (j + 1)
            ]
        out_ref[d, top : top + books, :] = code_rows
        out_ref[d, top + books :, :] = extra


def main_kernel(
    scale, books, me_ref, group_ref, cb_ref,
    loss_ref, gq_ref, gb_ref,
    cb_scr, q_scr, sorted_scr, dec_scr, s_scr, max_scr, sum_scr, total_scr, pg_scr,
):
    members = group_ref.shape[0]
    width, levels = cb_ref.shape
    sub_width = width // books
    rows = gq_ref.shape[0]
    blocks = width // LANES
    top = rows * blocks
    queries = members * rows
    me = me_ref[0, 0]
    cb_scr[...] = cb_ref[...].astype(jnp.float32)
    for j in range(blocks):
        q_scr[:, LANES * j : LANES * (j + 1)] = group_ref[
            :, rows * j : rows * (j + 1), :
        ].reshape(queries, LANES)
    sorted_scr[...] = jnp.dot(
        q_scr[...], order_table(width, books, False), preferred_element_type=jnp.float32
    ).astype(jnp.bfloat16)

    def decode(t):
        for side in range(2):
            codes = (
                group_ref[2 * t + side, top : top + books, :]
                .astype(jnp.float32)
                .astype(jnp.int32)
            )
            for g in range(books // 8):
                index = codes[8 * g : 8 * g + 8, :]
                inner = index & (LANES - 1)
                upper = index >= LANES
                for two in range(sub_width // 2):
                    tiles = []
                    for c in (2 * two, 2 * two + 1):
                        at = c * books + 8 * g
                        low = jnp.take_along_axis(cb_scr[at : at + 8, :LANES], inner, axis=1)
                        high = jnp.take_along_axis(cb_scr[at : at + 8, LANES:], inner, axis=1)
                        tiles.append(jnp.where(upper, high, low))
                    at = 8 * sub_width * g + 16 * two
                    dec_scr[t, at : at + 16, LANES * side : LANES * side + LANES] = (
                        jnp.concatenate(tiles, axis=0).astype(jnp.bfloat16)
                    )

    def score(t):
        both = jnp.dot(sorted_scr[...], dec_scr[t], preferred_element_type=jnp.float32)
        for r in range(0, queries, 32):
            left = both[r : r + 32, :LANES] * scale
            right = both[r : r + 32, LANES:] * scale
            s_scr[2 * t, r : r + 32, :] = left
            s_scr[2 * t + 1, r : r + 32, :] = right
            newest = jnp.maximum(left, right)
            if t > 0:
                before = max_scr[r : r + 32, :]
                newest = jnp.maximum(newest, before)
            total = jnp.exp(left - newest) + jnp.exp(right - newest)
            if t > 0:
                total = total + sum_scr[r : r + 32, :] * jnp.exp(before - newest)
            max_scr[r : r + 32, :] = newest
            sum_scr[r : r + 32, :] = total

    for t in range(members // 2):
        decode(t)
        score(t)

    highest = max_scr[...]
    row_max = jnp.max(highest, axis=1, keepdims=True)
    total = jnp.sum(sum_scr[...] * jnp.exp(highest - row_max), axis=1, keepdims=True)
    total_scr[...] = jnp.broadcast_to(row_max + jnp.log(total), (queries, LANES))

    def extras(block):
        weight = block[:, 0:1] + block[:, 1:2] + block[:, 2:3]
        return weight, block[:, 3:4], block[:, 4:5]

    extra = group_ref[:, top + books :, :].reshape(queries, LANES).astype(jnp.float32)
    weight, block, place = extras(extra)
    here = me.astype(jnp.float32)
    lane = lax.broadcasted_iota(jnp.int32, (queries, LANES), 1).astype(jnp.float32)
    is_positive = jnp.where((block == here) & (place == lane), 1.0, 0.0)
    coefficient = (
        weight * (jnp.exp(s_scr[me] - total_scr[...]) - is_positive) * scale
    ).astype(jnp.bfloat16)
    pg_scr[...] = lax.dot_general(
        q_scr[...], coefficient, (((0,), (0,)), ((), ())), preferred_element_type=jnp.float32
    )

    own_codes = group_ref[me, top : top + books, :].astype(jnp.float32)
    level = lax.broadcasted_iota(jnp.int32, (levels, LANES), 0).astype(jnp.float32)
    level = level.astype(jnp.bfloat16)
    one = jnp.ones((16, LANES), jnp.bfloat16)
    zero = jnp.zeros((16, LANES), jnp.bfloat16)
    pair_rows = 2 * sub_width
    upper = lax.broadcasted_iota(jnp.int32, (pair_rows, LANES), 0) < sub_width
    ready = []
    for m in range(0, books, 2):
        tables = []
        for h in range(2):
            row = jnp.broadcast_to(own_codes[m + h : m + h + 1, :], (16, LANES)).astype(
                jnp.bfloat16
            )
            tables.append(
                jnp.concatenate(
                    [
                        jnp.where(row == level[16 * j : 16 * j + 16, :], one, zero)
                        for j in range(levels // 16)
                    ],
                    axis=0,
                )
            )
        terms = pg_scr[sub_width * m : sub_width * m + pair_rows, :]
        high = terms.astype(jnp.bfloat16).astype(jnp.float32)
        parts = [
            jnp.concatenate([jnp.where(upper, x, 0.0), jnp.where(upper, 0.0, x)], axis=1)
            for x in (high, terms - high)
        ]
        sums = lax.dot_general(
            jnp.concatenate(parts, axis=0).astype(jnp.bfloat16),
            jnp.concatenate(tables, axis=1),
            (((1,), (1,)), ((), ())),
            preferred_element_type=jnp.float32,
        )
        ready.append(sums[:pair_rows] + sums[pair_rows:])
        if m % 4 == 2:
            at = sub_width * (m - 2)
            both = jnp.concatenate(ready, axis=0).astype(jnp.bfloat16)
            for j in range(levels // LANES):
                gb_ref[j, at : at + 2 * pair_rows, :] = both[:, LANES * j : LANES * (j + 1)]
            ready = []

    own = pl.ds(pl.multiple_of(me * rows, rows), rows)
    weight, block, place = extras(group_ref[me, top + books :, :].astype(jnp.float32))
    own_total = total_scr[own, :]
    own_lane = lax.broadcasted_iota(jnp.int32, (rows, LANES), 1).astype(jnp.float32)
    chosen = jnp.zeros((rows, LANES), jnp.float32)
    grad = jnp.zeros((rows, width), jnp.float32)
    for t in range(members // 2):
        parts = []
        for d in (2 * t, 2 * t + 1):
            scores = s_scr[d, own, :]
            hit = (block == float(d)) & (place == own_lane)
            chosen = chosen + jnp.where(hit, scores, 0.0)
            parts.append(
                weight * (jnp.exp(scores - own_total) - jnp.where(hit, 1.0, 0.0)) * scale
            )
        grad = grad + lax.dot_general(
            jnp.concatenate(parts, axis=1).astype(jnp.bfloat16),
            dec_scr[t],
            (((1,), (1,)), ((), ())),
            preferred_element_type=jnp.float32,
        )
    gq_ref[...] = grad
    loss = weight * (own_total - jnp.sum(chosen, axis=1, keepdims=True))
    diagonal = lax.broadcasted_iota(jnp.int32, (rows, LANES), 0).astype(jnp.float32) == own_lane
    loss_ref[...] = jnp.sum(jnp.where(diagonal, loss, 0.0), axis=0, keepdims=True)[:, :rows]


def restore_kernel(books, grad_ref, out_ref):
    rows, width = grad_ref.shape
    grad = grad_ref[...]
    first = grad.astype(jnp.bfloat16).astype(jnp.float32)
    second = (grad - first).astype(jnp.bfloat16).astype(jnp.float32)
    third = grad - first - second
    restored = jnp.dot(
        jnp.concatenate([first, second, third], axis=0).astype(jnp.bfloat16),
        order_table(width, books, True),
        preferred_element_type=jnp.float32,
    )
    out_ref[...] = restored[:rows] + restored[rows : 2 * rows] + restored[2 * rows :]


def spread(block, axis):
    copies = jnp.broadcast_to(block[None], (lax.axis_size(axis),) + block.shape)
    return lax.all_to_all(copies, axis, 0, 0)


def per_device(queries, passage_codes, codebooks, positives, loss_weight):
    rows, width = queries.shape
    books = passage_codes.shape[1]
    sub_width, levels = codebooks.shape[1:]
    members = lax.axis_size("db")
    plane = lax.axis_size(PLANE)
    pack_rows = rows * (width // LANES) + books + rows
    scale = 2.5 / math.sqrt(width)
    pack = pl.pallas_call(
        pack_kernel,
        out_shape=jax.ShapeDtypeStruct((members, pack_rows, LANES), jnp.bfloat16),
        compiler_params=pltpu.CompilerParams(vmem_limit_bytes=8 * 1024 * 1024),
        name="pack",
    )(queries, passage_codes.T, loss_weight.reshape(1, rows), positives.reshape(1, rows))
    group = lax.all_to_all(pack, "db", 0, 0)
    me = lax.axis_index("db").astype(jnp.int32).reshape(1, 1)
    loss, grad_queries, book_part = pl.pallas_call(
        functools.partial(main_kernel, scale, books),
        out_shape=(
            jax.ShapeDtypeStruct((1, rows), jnp.float32),
            jax.ShapeDtypeStruct((rows, width), jnp.float32),
            jax.ShapeDtypeStruct((levels // LANES, width, LANES), jnp.bfloat16),
        ),
        in_specs=[pl.BlockSpec(memory_space=pltpu.SMEM)]
        + [pl.BlockSpec(memory_space=pltpu.VMEM)] * 2,
        scratch_shapes=[
            pltpu.VMEM((width, levels), jnp.float32),
            pltpu.VMEM((members * rows, width), jnp.bfloat16),
            pltpu.VMEM((members * rows, width), jnp.bfloat16),
            pltpu.VMEM((members // 2, width, 2 * LANES), jnp.bfloat16),
            pltpu.VMEM((members, members * rows, LANES), jnp.float32),
            pltpu.VMEM((members * rows, LANES), jnp.float32),
            pltpu.VMEM((members * rows, LANES), jnp.float32),
            pltpu.VMEM((members * rows, LANES), jnp.float32),
            pltpu.VMEM((width, LANES), jnp.float32),
        ],
        compiler_params=pltpu.CompilerParams(vmem_limit_bytes=24 * 1024 * 1024),
        name="core",
    )(me, group, codebooks.transpose(1, 0, 2).reshape(width, levels))
    grad_queries = pl.pallas_call(
        functools.partial(restore_kernel, books),
        out_shape=jax.ShapeDtypeStruct((rows, width), jnp.float32),
        compiler_params=pltpu.CompilerParams(vmem_limit_bytes=8 * 1024 * 1024),
        name="restore",
    )(grad_queries)
    part = lax.all_to_all(book_part.reshape(plane, -1, LANES), PLANE, 0, 0)
    part = jnp.sum(part.astype(jnp.float32), axis=0).astype(jnp.bfloat16)
    part = spread(part, "far")
    part = jnp.sum(part.astype(jnp.float32), axis=0).astype(jnp.bfloat16)
    part = spread(part, PLANE).astype(jnp.float32)
    book_total = part.reshape(-1, books, sub_width, LANES).transpose(1, 2, 0, 3)
    return loss.reshape(rows), grad_queries, book_total.reshape(books, sub_width, levels)


def solution(mesh):
    lines, stacks = mesh.devices.shape
    fine = Mesh(mesh.devices.reshape(lines, 2, stacks // 4, 2), WHOLE)
    return jax.shard_map(
        per_device,
        mesh=fine,
        in_specs=(P(WHOLE, None), P(WHOLE, None), P(), P(WHOLE), P(WHOLE)),
        out_specs=(P(WHOLE), P(WHOLE, None), P()),
        check_vma=False,
    )
```

```python
import functools
import math

import jax
import jax.numpy as jnp
from jax import lax
from jax.experimental import pallas as pl
from jax.experimental.pallas import tpu as pltpu
from jax.sharding import Mesh
from jax.sharding import PartitionSpec as P

LANES = 128
PLANE = ("db", "near", "pair")
WHOLE = ("db", "near", "far", "pair")


def order_table(width, books):
    sub_width = width // books
    row = lax.broadcasted_iota(jnp.int32, (width, width), 0)
    place = lax.broadcasted_iota(jnp.int32, (1, width), 1)
    inner = place % (8 * sub_width)
    source = (place // (8 * sub_width) * 8 + inner % 8) * sub_width + inner // 8
    return jnp.where(row == source, 1.0, 0.0).astype(jnp.bfloat16)


def pack_kernel(queries_ref, codes_ref, weight_ref, positive_ref, out_ref):
    rows, width = queries_ref.shape
    books = codes_ref.shape[0]
    top = rows * (width // LANES)
    code_rows = codes_ref[...].astype(jnp.float32).astype(jnp.bfloat16)
    spot = lax.broadcasted_iota(jnp.int32, (rows, rows), 0)
    lane = lax.broadcasted_iota(jnp.int32, (rows, rows), 1)

    def column(row):
        spread_row = jnp.broadcast_to(row, (rows, rows))
        return jnp.sum(jnp.where(spot == lane, spread_row, 0.0), axis=1, keepdims=True)

    weight = column(weight_ref[...])
    positive = positive_ref[...]
    first = weight.astype(jnp.bfloat16).astype(jnp.float32)
    second = (weight - first).astype(jnp.bfloat16).astype(jnp.float32)
    third = weight - first - second
    block = column((positive // LANES).astype(jnp.float32))
    place = column((positive % LANES).astype(jnp.float32))
    wide = lax.broadcasted_iota(jnp.int32, (rows, LANES), 1)
    extra = jnp.zeros((rows, LANES), jnp.float32)
    for j, value in enumerate((first, second, third, block, place)):
        extra = jnp.where(wide == j, value, extra)
    extra = extra.astype(jnp.bfloat16)
    for d in range(out_ref.shape[0]):
        for j in range(width // LANES):
            out_ref[d, rows * j : rows * (j + 1), :] = queries_ref[
                :, LANES * j : LANES * (j + 1)
            ]
        out_ref[d, top : top + books, :] = code_rows
        out_ref[d, top + books :, :] = extra


def main_kernel(
    scale, books, me_ref, group_ref, cb_ref,
    loss_ref, gq_ref, gb_ref,
    cb_scr, q_scr, table_scr, sorted_scr, dec_scr, s_scr, max_scr, sum_scr, total_scr, pg_scr,
):
    members = group_ref.shape[0]
    width, levels = cb_ref.shape
    sub_width = width // books
    rows = gq_ref.shape[0]
    blocks = width // LANES
    top = rows * blocks
    queries = members * rows
    me = me_ref[0, 0]
    cb_scr[...] = cb_ref[...].astype(jnp.float32)
    for j in range(blocks):
        q_scr[:, LANES * j : LANES * (j + 1)] = group_ref[
            :, rows * j : rows * (j + 1), :
        ].reshape(queries, LANES)
    table_scr[...] = order_table(width, books)
    sorted_scr[...] = jnp.dot(
        q_scr[...], table_scr[...], preferred_element_type=jnp.float32
    ).astype(jnp.bfloat16)

    def decode(t):
        for side in range(2):
            codes = (
                group_ref[2 * t + side, top : top + books, :]
                .astype(jnp.float32)
                .astype(jnp.int32)
            )
            for g in range(books // 8):
                index = codes[8 * g : 8 * g + 8, :]
                inner = index & (LANES - 1)
                upper = index >= LANES
                for two in range(sub_width // 2):
                    tiles = []
                    for c in (2 * two, 2 * two + 1):
                        at = c * books + 8 * g
                        low = jnp.take_along_axis(cb_scr[at : at + 8, :LANES], inner, axis=1)
                        high = jnp.take_along_axis(cb_scr[at : at + 8, LANES:], inner, axis=1)
                        tiles.append(jnp.where(upper, high, low))
                    at = 8 * sub_width * g + 16 * two
                    dec_scr[t, at : at + 16, LANES * side : LANES * side + LANES] = (
                        jnp.concatenate(tiles, axis=0).astype(jnp.bfloat16)
                    )

    def score(t):
        both = jnp.dot(sorted_scr[...], dec_scr[t], preferred_element_type=jnp.float32)
        for r in range(0, queries, 32):
            left = both[r : r + 32, :LANES] * scale
            right = both[r : r + 32, LANES:] * scale
            s_scr[2 * t, r : r + 32, :] = left
            s_scr[2 * t + 1, r : r + 32, :] = right
            newest = jnp.maximum(left, right)
            if t > 0:
                before = max_scr[r : r + 32, :]
                newest = jnp.maximum(newest, before)
            total = jnp.exp(left - newest) + jnp.exp(right - newest)
            if t > 0:
                total = total + sum_scr[r : r + 32, :] * jnp.exp(before - newest)
            max_scr[r : r + 32, :] = newest
            sum_scr[r : r + 32, :] = total

    for t in range(members // 2):
        decode(t)
        score(t)

    highest = max_scr[...]
    row_max = jnp.max(highest, axis=1, keepdims=True)
    total = jnp.sum(sum_scr[...] * jnp.exp(highest - row_max), axis=1, keepdims=True)
    total_scr[...] = jnp.broadcast_to(row_max + jnp.log(total), (queries, LANES))

    def extras(block):
        weight = block[:, 0:1] + block[:, 1:2] + block[:, 2:3]
        return weight, block[:, 3:4], block[:, 4:5]

    extra = group_ref[:, top + books :, :].reshape(queries, LANES).astype(jnp.float32)
    weight, block, place = extras(extra)
    here = me.astype(jnp.float32)
    lane = lax.broadcasted_iota(jnp.int32, (queries, LANES), 1).astype(jnp.float32)
    is_positive = jnp.where((block == here) & (place == lane), 1.0, 0.0)
    coefficient = (
        weight * (jnp.exp(s_scr[me] - total_scr[...]) - is_positive) * scale
    ).astype(jnp.bfloat16)
    pg_scr[...] = lax.dot_general(
        sorted_scr[...],
        coefficient,
        (((0,), (0,)), ((), ())),
        preferred_element_type=jnp.float32,
    ).astype(jnp.bfloat16)

    own_codes = group_ref[me, top : top + books, :].astype(jnp.float32)
    level = lax.broadcasted_iota(jnp.int32, (levels, LANES), 0).astype(jnp.float32)
    level = level.astype(jnp.bfloat16)
    one = jnp.ones((16, LANES), jnp.bfloat16)
    zero = jnp.zeros((16, LANES), jnp.bfloat16)
    part_rows = 8 * sub_width
    spot = lax.broadcasted_iota(jnp.int32, (part_rows, LANES), 0) % 8
    spot = spot.astype(jnp.float32).astype(jnp.bfloat16)
    blank = jnp.zeros((part_rows, LANES), jnp.bfloat16)
    for g in range(books // 8):
        tables = []
        parts = []
        terms = pg_scr[part_rows * g : part_rows * (g + 1), :]
        for i in range(8):
            m = 8 * g + i
            row = jnp.broadcast_to(own_codes[m : m + 1, :], (16, LANES)).astype(jnp.bfloat16)
            tables.append(
                jnp.concatenate(
                    [
                        jnp.where(row == level[16 * j : 16 * j + 16, :], one, zero)
                        for j in range(levels // 16)
                    ],
                    axis=0,
                )
            )
            parts.append(jnp.where(spot == jnp.full_like(spot, i), terms, blank))
        sums = lax.dot_general(
            jnp.concatenate(parts, axis=1),
            jnp.concatenate(tables, axis=1),
            (((1,), (1,)), ((), ())),
            preferred_element_type=jnp.float32,
        ).astype(jnp.bfloat16)
        for c in range(sub_width):
            at = c * books + 8 * g
            for j in range(levels // LANES):
                gb_ref[j, at : at + 8, :] = sums[8 * c : 8 * c + 8, LANES * j : LANES * (j + 1)]

    own = pl.ds(pl.multiple_of(me * rows, rows), rows)
    weight, block, place = extras(group_ref[me, top + books :, :].astype(jnp.float32))
    own_total = total_scr[own, :]
    own_lane = lax.broadcasted_iota(jnp.int32, (rows, LANES), 1).astype(jnp.float32)
    chosen = jnp.zeros((rows, LANES), jnp.float32)
    grad = jnp.zeros((rows, width), jnp.float32)
    for t in range(members // 2):
        parts = []
        for d in (2 * t, 2 * t + 1):
            scores = s_scr[d, own, :]
            hit = (block == float(d)) & (place == own_lane)
            chosen = chosen + jnp.where(hit, scores, 0.0)
            parts.append(
                weight * (jnp.exp(scores - own_total) - jnp.where(hit, 1.0, 0.0)) * scale
            )
        grad = grad + lax.dot_general(
            jnp.concatenate(parts, axis=1).astype(jnp.bfloat16),
            dec_scr[t],
            (((1,), (1,)), ((), ())),
            preferred_element_type=jnp.float32,
        )
    first = grad.astype(jnp.bfloat16).astype(jnp.float32)
    second = (grad - first).astype(jnp.bfloat16).astype(jnp.float32)
    third = grad - first - second
    restored = lax.dot_general(
        jnp.concatenate([first, second, third], axis=0).astype(jnp.bfloat16),
        table_scr[...],
        (((1,), (1,)), ((), ())),
        preferred_element_type=jnp.float32,
    )
    gq_ref[...] = restored[:rows] + restored[rows : 2 * rows] + restored[2 * rows :]
    loss = weight * (own_total - jnp.sum(chosen, axis=1, keepdims=True))
    diagonal = lax.broadcasted_iota(jnp.int32, (rows, LANES), 0).astype(jnp.float32) == own_lane
    loss_ref[...] = jnp.sum(jnp.where(diagonal, loss, 0.0), axis=0, keepdims=True)[:, :rows]


def widen_kernel(part_ref, out_ref):
    for j in range(part_ref.shape[0]):
        out_ref[:, LANES * j : LANES * (j + 1)] = part_ref[j].astype(jnp.float32)


def spread(block, axis):
    copies = jnp.broadcast_to(block[None], (lax.axis_size(axis),) + block.shape)
    return lax.all_to_all(copies, axis, 0, 0)


def per_device(queries, passage_codes, codebooks, positives, loss_weight):
    rows, width = queries.shape
    books = passage_codes.shape[1]
    sub_width, levels = codebooks.shape[1:]
    members = lax.axis_size("db")
    plane = lax.axis_size(PLANE)
    pack_rows = rows * (width // LANES) + books + rows
    scale = 2.5 / math.sqrt(width)
    pack = pl.pallas_call(
        pack_kernel,
        out_shape=jax.ShapeDtypeStruct((members, pack_rows, LANES), jnp.bfloat16),
        name="pack",
    )(queries, passage_codes.T, loss_weight.reshape(1, rows), positives.reshape(1, rows))
    group = lax.all_to_all(pack, "db", 0, 0)
    me = lax.axis_index("db").astype(jnp.int32).reshape(1, 1)
    loss, grad_queries, book_part = pl.pallas_call(
        functools.partial(main_kernel, scale, books),
        out_shape=(
            jax.ShapeDtypeStruct((1, rows), jnp.float32),
            jax.ShapeDtypeStruct((rows, width), jnp.float32),
            jax.ShapeDtypeStruct((levels // LANES, width, LANES), jnp.bfloat16),
        ),
        in_specs=[pl.BlockSpec(memory_space=pltpu.SMEM)]
        + [pl.BlockSpec(memory_space=pltpu.VMEM)] * 2,
        scratch_shapes=[
            pltpu.VMEM((width, levels), jnp.float32),
            pltpu.VMEM((members * rows, width), jnp.bfloat16),
            pltpu.VMEM((width, width), jnp.bfloat16),
            pltpu.VMEM((members * rows, width), jnp.bfloat16),
            pltpu.VMEM((members // 2, width, 2 * LANES), jnp.bfloat16),
            pltpu.VMEM((members, members * rows, LANES), jnp.float32),
            pltpu.VMEM((members * rows, LANES), jnp.float32),
            pltpu.VMEM((members * rows, LANES), jnp.float32),
            pltpu.VMEM((members * rows, LANES), jnp.float32),
            pltpu.VMEM((width, LANES), jnp.bfloat16),
        ],
        compiler_params=pltpu.CompilerParams(vmem_limit_bytes=24 * 1024 * 1024),
        name="core",
    )(me, group, codebooks.transpose(1, 0, 2).reshape(width, levels))
    part = lax.all_to_all(book_part.reshape(plane, -1, LANES), PLANE, 0, 0)
    part = jnp.sum(part.astype(jnp.float32), axis=0).astype(jnp.bfloat16)
    part = spread(part, "far")
    part = jnp.sum(part.astype(jnp.float32), axis=0).astype(jnp.bfloat16)
    part = spread(part, PLANE).reshape(-1, width, LANES)
    book_total = pl.pallas_call(
        widen_kernel,
        out_shape=jax.ShapeDtypeStruct((width, levels), jnp.float32),
        compiler_params=pltpu.CompilerParams(vmem_limit_bytes=8 * 1024 * 1024),
        name="widen",
    )(part)
    book_total = book_total.reshape(sub_width, books, levels).transpose(1, 0, 2)
    return loss.reshape(rows), grad_queries, book_total


def solution(mesh):
    lines, stacks = mesh.devices.shape
    fine = Mesh(mesh.devices.reshape(lines, 2, stacks // 4, 2), WHOLE)
    return jax.shard_map(
        per_device,
        mesh=fine,
        in_specs=(P(WHOLE, None), P(WHOLE, None), P(), P(WHOLE), P(WHOLE)),
        out_specs=(P(WHOLE), P(WHOLE, None), P()),
        check_vma=False,
    )
```

```python
import functools
import math

import jax
import jax.numpy as jnp
from jax import lax
from jax.experimental import pallas as pl
from jax.experimental.pallas import tpu as pltpu
from jax.sharding import Mesh
from jax.sharding import PartitionSpec as P

LANES = 128
PLANE = ("db", "near", "pair")
WHOLE = ("db", "near", "far", "pair")


def order_table(width, books):
    sub_width = width // books
    row = lax.broadcasted_iota(jnp.int32, (width, width), 0)
    place = lax.broadcasted_iota(jnp.int32, (1, width), 1)
    inner = place % (8 * sub_width)
    source = (place // (8 * sub_width) * 8 + inner % 8) * sub_width + inner // 8
    return jnp.where(row == source, 1.0, 0.0).astype(jnp.bfloat16)


def pack_kernel(queries_ref, codes_ref, weight_ref, positive_ref, out_ref):
    rows, width = queries_ref.shape
    books = codes_ref.shape[0]
    top = rows * (width // LANES)
    sorted_rows = jnp.dot(
        queries_ref[...], order_table(width, books), preferred_element_type=jnp.float32
    ).astype(jnp.bfloat16)
    code_rows = codes_ref[...].astype(jnp.float32).astype(jnp.bfloat16)
    spot = lax.broadcasted_iota(jnp.int32, (rows, rows), 0)
    lane = lax.broadcasted_iota(jnp.int32, (rows, rows), 1)

    def column(row):
        spread_row = jnp.broadcast_to(row, (rows, rows))
        return jnp.sum(jnp.where(spot == lane, spread_row, 0.0), axis=1, keepdims=True)

    weight = column(weight_ref[...])
    positive = positive_ref[...]
    first = weight.astype(jnp.bfloat16).astype(jnp.float32)
    second = (weight - first).astype(jnp.bfloat16).astype(jnp.float32)
    third = weight - first - second
    block = column((positive // LANES).astype(jnp.float32))
    place = column((positive % LANES).astype(jnp.float32))
    wide = lax.broadcasted_iota(jnp.int32, (rows, LANES), 1)
    extra = jnp.zeros((rows, LANES), jnp.float32)
    for j, value in enumerate((first, second, third, block, place)):
        extra = jnp.where(wide == j, value, extra)
    extra = extra.astype(jnp.bfloat16)
    for d in range(out_ref.shape[0]):
        for j in range(width // LANES):
            out_ref[d, rows * j : rows * (j + 1), :] = sorted_rows[:, LANES * j : LANES * (j + 1)]
        out_ref[d, top : top + books, :] = code_rows
        out_ref[d, top + books :, :] = extra


def main_kernel(
    scale, books, me_ref, group_ref, cb_ref,
    loss_ref, gq_ref, gb_ref,
    cb_scr, sorted_scr, dec_scr, s_scr, max_scr, sum_scr, total_scr, pg_scr,
):
    members = group_ref.shape[0]
    width, levels = cb_ref.shape
    sub_width = width // books
    rows = gq_ref.shape[0]
    blocks = width // LANES
    top = rows * blocks
    queries = members * rows
    me = me_ref[0, 0]
    cb_scr[...] = cb_ref[...].astype(jnp.float32)
    for j in range(blocks):
        sorted_scr[:, LANES * j : LANES * (j + 1)] = group_ref[
            :, rows * j : rows * (j + 1), :
        ].reshape(queries, LANES)
    done = []

    def decode(t):
        for side in range(2):
            codes = (
                group_ref[2 * t + side, top : top + books, :]
                .astype(jnp.float32)
                .astype(jnp.int32)
            )
            for g in range(books // 8):
                index = codes[8 * g : 8 * g + 8, :]
                inner = index & (LANES - 1)
                upper = index >= LANES
                if len(done) >= 4:
                    inner = inner + (done[-4] * 0.0).astype(jnp.int32)
                for two in range(sub_width // 2):
                    tiles = []
                    for c in (2 * two, 2 * two + 1):
                        at = c * books + 8 * g
                        low = jnp.take_along_axis(cb_scr[at : at + 8, :LANES], inner, axis=1)
                        high = jnp.take_along_axis(cb_scr[at : at + 8, LANES:], inner, axis=1)
                        tiles.append(jnp.where(upper, high, low))
                    if two == 0:
                        done.append(tiles[0])
                    at = 8 * sub_width * g + 16 * two
                    dec_scr[t, at : at + 16, LANES * side : LANES * side + LANES] = (
                        jnp.concatenate(tiles, axis=0).astype(jnp.bfloat16)
                    )

    def score(t):
        both = jnp.dot(sorted_scr[...], dec_scr[t], preferred_element_type=jnp.float32)
        for r in range(0, queries, 32):
            left = both[r : r + 32, :LANES] * scale
            right = both[r : r + 32, LANES:] * scale
            s_scr[2 * t, r : r + 32, :] = left
            s_scr[2 * t + 1, r : r + 32, :] = right
            newest = jnp.maximum(left, right)
            if t > 0:
                before = max_scr[r : r + 32, :]
                newest = jnp.maximum(newest, before)
            total = jnp.exp(left - newest) + jnp.exp(right - newest)
            if t > 0:
                total = total + sum_scr[r : r + 32, :] * jnp.exp(before - newest)
            max_scr[r : r + 32, :] = newest
            sum_scr[r : r + 32, :] = total

    for t in range(members // 2):
        decode(t)
        score(t)

    highest = max_scr[...]
    row_max = jnp.max(highest, axis=1, keepdims=True)
    total = jnp.sum(sum_scr[...] * jnp.exp(highest - row_max), axis=1, keepdims=True)
    total_scr[...] = jnp.broadcast_to(row_max + jnp.log(total), (queries, LANES))

    def extras(block):
        weight = block[:, 0:1] + block[:, 1:2] + block[:, 2:3]
        return weight, block[:, 3:4], block[:, 4:5]

    extra = group_ref[:, top + books :, :].reshape(queries, LANES).astype(jnp.float32)
    weight, block, place = extras(extra)
    here = me.astype(jnp.float32)
    lane = lax.broadcasted_iota(jnp.int32, (queries, LANES), 1).astype(jnp.float32)
    is_positive = jnp.where((block == here) & (place == lane), 1.0, 0.0)
    coefficient = (
        weight * (jnp.exp(s_scr[me] - total_scr[...]) - is_positive) * scale
    ).astype(jnp.bfloat16)
    pg_scr[...] = lax.dot_general(
        sorted_scr[...],
        coefficient,
        (((0,), (0,)), ((), ())),
        preferred_element_type=jnp.float32,
    ).astype(jnp.bfloat16)

    own_codes = group_ref[me, top : top + books, :].astype(jnp.float32)
    level = lax.broadcasted_iota(jnp.int32, (levels, LANES), 0).astype(jnp.float32)
    level = level.astype(jnp.bfloat16)
    one = jnp.ones((16, LANES), jnp.bfloat16)
    zero = jnp.zeros((16, LANES), jnp.bfloat16)
    part_rows = 8 * sub_width
    spot = lax.broadcasted_iota(jnp.int32, (part_rows, LANES), 0) % 8
    spot = spot.astype(jnp.float32).astype(jnp.bfloat16)
    blank = jnp.zeros((part_rows, LANES), jnp.bfloat16)
    for g in range(books // 8):
        tables = []
        parts = []
        terms = pg_scr[part_rows * g : part_rows * (g + 1), :]
        for i in range(8):
            m = 8 * g + i
            row = jnp.broadcast_to(own_codes[m : m + 1, :], (16, LANES)).astype(jnp.bfloat16)
            tables.append(
                jnp.concatenate(
                    [
                        jnp.where(row == level[16 * j : 16 * j + 16, :], one, zero)
                        for j in range(levels // 16)
                    ],
                    axis=0,
                )
            )
            parts.append(jnp.where(spot == jnp.full_like(spot, i), terms, blank))
        sums = lax.dot_general(
            jnp.concatenate(parts, axis=1),
            jnp.concatenate(tables, axis=1),
            (((1,), (1,)), ((), ())),
            preferred_element_type=jnp.float32,
        ).astype(jnp.bfloat16)
        for c in range(sub_width):
            at = c * books + 8 * g
            for j in range(levels // LANES):
                gb_ref[j, at : at + 8, :] = sums[8 * c : 8 * c + 8, LANES * j : LANES * (j + 1)]

    own = pl.ds(pl.multiple_of(me * rows, rows), rows)
    weight, block, place = extras(group_ref[me, top + books :, :].astype(jnp.float32))
    own_total = total_scr[own, :]
    own_lane = lax.broadcasted_iota(jnp.int32, (rows, LANES), 1).astype(jnp.float32)
    chosen = jnp.zeros((rows, LANES), jnp.float32)
    grad = jnp.zeros((rows, width), jnp.float32)
    for t in range(members // 2):
        parts = []
        for d in (2 * t, 2 * t + 1):
            scores = s_scr[d, own, :]
            hit = (block == float(d)) & (place == own_lane)
            chosen = chosen + jnp.where(hit, scores, 0.0)
            parts.append(
                weight * (jnp.exp(scores - own_total) - jnp.where(hit, 1.0, 0.0)) * scale
            )
        grad = grad + lax.dot_general(
            jnp.concatenate(parts, axis=1).astype(jnp.bfloat16),
            dec_scr[t],
            (((1,), (1,)), ((), ())),
            preferred_element_type=jnp.float32,
        )
    first = grad.astype(jnp.bfloat16).astype(jnp.float32)
    second = (grad - first).astype(jnp.bfloat16).astype(jnp.float32)
    third = grad - first - second
    restored = lax.dot_general(
        jnp.concatenate([first, second, third], axis=0).astype(jnp.bfloat16),
        order_table(width, books),
        (((1,), (1,)), ((), ())),
        preferred_element_type=jnp.float32,
    )
    gq_ref[...] = restored[:rows] + restored[rows : 2 * rows] + restored[2 * rows :]
    loss = weight * (own_total - jnp.sum(chosen, axis=1, keepdims=True))
    diagonal = lax.broadcasted_iota(jnp.int32, (rows, LANES), 0).astype(jnp.float32) == own_lane
    loss_ref[...] = jnp.sum(jnp.where(diagonal, loss, 0.0), axis=0, keepdims=True)[:, :rows]


def widen_kernel(part_ref, out_ref):
    for j in range(part_ref.shape[0]):
        out_ref[:, LANES * j : LANES * (j + 1)] = part_ref[j].astype(jnp.float32)


def spread(block, axis):
    copies = jnp.broadcast_to(block[None], (lax.axis_size(axis),) + block.shape)
    return lax.all_to_all(copies, axis, 0, 0)


def per_device(queries, passage_codes, codebooks, positives, loss_weight):
    rows, width = queries.shape
    books = passage_codes.shape[1]
    sub_width, levels = codebooks.shape[1:]
    members = lax.axis_size("db")
    plane = lax.axis_size(PLANE)
    pack_rows = rows * (width // LANES) + books + rows
    scale = 2.5 / math.sqrt(width)
    pack = pl.pallas_call(
        pack_kernel,
        out_shape=jax.ShapeDtypeStruct((members, pack_rows, LANES), jnp.bfloat16),
        name="pack",
    )(queries, passage_codes.T, loss_weight.reshape(1, rows), positives.reshape(1, rows))
    group = lax.all_to_all(pack, "db", 0, 0)
    me = lax.axis_index("db").astype(jnp.int32).reshape(1, 1)
    loss, grad_queries, book_part = pl.pallas_call(
        functools.partial(main_kernel, scale, books),
        out_shape=(
            jax.ShapeDtypeStruct((1, rows), jnp.float32),
            jax.ShapeDtypeStruct((rows, width), jnp.float32),
            jax.ShapeDtypeStruct((levels // LANES, width, LANES), jnp.bfloat16),
        ),
        in_specs=[pl.BlockSpec(memory_space=pltpu.SMEM)]
        + [pl.BlockSpec(memory_space=pltpu.VMEM)] * 2,
        scratch_shapes=[
            pltpu.VMEM((width, levels), jnp.float32),
            pltpu.VMEM((members * rows, width), jnp.bfloat16),
            pltpu.VMEM((members // 2, width, 2 * LANES), jnp.bfloat16),
            pltpu.VMEM((members, members * rows, LANES), jnp.float32),
            pltpu.VMEM((members * rows, LANES), jnp.float32),
            pltpu.VMEM((members * rows, LANES), jnp.float32),
            pltpu.VMEM((members * rows, LANES), jnp.float32),
            pltpu.VMEM((width, LANES), jnp.bfloat16),
        ],
        compiler_params=pltpu.CompilerParams(vmem_limit_bytes=24 * 1024 * 1024),
        name="core",
    )(me, group, codebooks.transpose(1, 0, 2).reshape(width, levels))
    part = lax.all_to_all(book_part.reshape(plane, -1, LANES), PLANE, 0, 0)
    part = jnp.sum(part.astype(jnp.float32), axis=0).astype(jnp.bfloat16)
    part = spread(part, "far")
    part = jnp.sum(part.astype(jnp.float32), axis=0).astype(jnp.bfloat16)
    part = spread(part, PLANE).reshape(-1, width, LANES)
    book_total = pl.pallas_call(
        widen_kernel,
        out_shape=jax.ShapeDtypeStruct((width, levels), jnp.float32),
        compiler_params=pltpu.CompilerParams(vmem_limit_bytes=8 * 1024 * 1024),
        name="widen",
    )(part)
    book_total = book_total.reshape(sub_width, books, levels).transpose(1, 0, 2)
    return loss.reshape(rows), grad_queries, book_total


def solution(mesh):
    lines, stacks = mesh.devices.shape
    fine = Mesh(mesh.devices.reshape(lines, 2, stacks // 4, 2), WHOLE)
    return jax.shard_map(
        per_device,
        mesh=fine,
        in_specs=(P(WHOLE, None), P(WHOLE, None), P(), P(WHOLE), P(WHOLE)),
        out_specs=(P(WHOLE), P(WHOLE, None), P()),
        check_vma=False,
    )
```

```python
import functools
import math

import jax
import jax.numpy as jnp
from jax import lax
from jax.experimental import pallas as pl
from jax.experimental.pallas import tpu as pltpu
from jax.sharding import Mesh
from jax.sharding import PartitionSpec as P

LANES = 128
PLANE = ("db", "near", "pair")
WHOLE = ("db", "near", "far", "pair")


def order_table(width, books, start, count, kind):
    sub_width = width // books
    row = lax.broadcasted_iota(jnp.int32, (width, count), 0).astype(kind)
    place = lax.broadcasted_iota(jnp.int32, (1, count), 1) + start
    inner = place % (8 * sub_width)
    source = (place // (8 * sub_width) * 8 + inner % 8) * sub_width + inner // 8
    return jnp.where(row == source.astype(kind), 1.0, 0.0).astype(jnp.bfloat16)


def pack_kernel(queries_ref, codes_ref, weight_ref, positive_ref, out_ref):
    rows, width = queries_ref.shape
    books = codes_ref.shape[0]
    top = rows * (width // LANES)
    code_rows = codes_ref[...].astype(jnp.float32).astype(jnp.bfloat16)
    spot = lax.broadcasted_iota(jnp.int32, (rows, rows), 0)
    lane = lax.broadcasted_iota(jnp.int32, (rows, rows), 1)

    def column(row):
        spread_row = jnp.broadcast_to(row, (rows, rows))
        return jnp.sum(jnp.where(spot == lane, spread_row, 0.0), axis=1, keepdims=True)

    weight = column(weight_ref[...])
    positive = positive_ref[...]
    first = weight.astype(jnp.bfloat16).astype(jnp.float32)
    second = (weight - first).astype(jnp.bfloat16).astype(jnp.float32)
    third = weight - first - second
    block = column((positive // LANES).astype(jnp.float32))
    place = column((positive % LANES).astype(jnp.float32))
    wide = lax.broadcasted_iota(jnp.int32, (rows, LANES), 1)
    extra = jnp.zeros((rows, LANES), jnp.float32)
    for j, value in enumerate((first, second, third, block, place)):
        extra = jnp.where(wide == j, value, extra)
    extra = extra.astype(jnp.bfloat16)
    for d in range(out_ref.shape[0]):
        for j in range(width // LANES):
            out_ref[d, rows * j : rows * (j + 1), :] = queries_ref[
                :, LANES * j : LANES * (j + 1)
            ]
        out_ref[d, top : top + books, :] = code_rows
        out_ref[d, top + books :, :] = extra


def main_kernel(
    scale, books, me_ref, group_ref, cb_ref,
    loss_ref, gq_ref, gb_ref,
    cb_scr, q_scr, sorted_scr, dec_scr, s_scr, max_scr, sum_scr, total_scr, pg_scr,
):
    members = group_ref.shape[0]
    width, levels = cb_ref.shape
    sub_width = width // books
    rows = gq_ref.shape[0]
    blocks = width // LANES
    top = rows * blocks
    queries = members * rows
    me = me_ref[0, 0]
    cb_scr[...] = cb_ref[...].astype(jnp.float32)
    for j in range(blocks):
        q_scr[:, LANES * j : LANES * (j + 1)] = group_ref[
            :, rows * j : rows * (j + 1), :
        ].reshape(queries, LANES)
    span = 2 * LANES
    for j in range(0, width, span):
        sorted_scr[:, j : j + span] = jnp.dot(
            q_scr[...],
            order_table(width, books, j, span, jnp.int32),
            preferred_element_type=jnp.float32,
        ).astype(jnp.bfloat16)
    done = []

    def decode(t):
        for side in range(2):
            codes = (
                group_ref[2 * t + side, top : top + books, :]
                .astype(jnp.float32)
                .astype(jnp.int32)
            )
            for g in range(books // 8):
                index = codes[8 * g : 8 * g + 8, :]
                inner = index & (LANES - 1)
                upper = index >= LANES
                if len(done) >= 4:
                    inner = inner + (done[-4] * 0.0).astype(jnp.int32)
                for two in range(sub_width // 2):
                    tiles = []
                    for c in (2 * two, 2 * two + 1):
                        at = c * books + 8 * g
                        low = jnp.take_along_axis(cb_scr[at : at + 8, :LANES], inner, axis=1)
                        high = jnp.take_along_axis(cb_scr[at : at + 8, LANES:], inner, axis=1)
                        tiles.append(jnp.where(upper, high, low))
                    if two == 0:
                        done.append(tiles[0])
                    at = 8 * sub_width * g + 16 * two
                    dec_scr[t, at : at + 16, LANES * side : LANES * side + LANES] = (
                        jnp.concatenate(tiles, axis=0).astype(jnp.bfloat16)
                    )

    def score(t):
        both = jnp.dot(sorted_scr[...], dec_scr[t], preferred_element_type=jnp.float32)
        for r in range(0, queries, 32):
            left = both[r : r + 32, :LANES] * scale
            right = both[r : r + 32, LANES:] * scale
            s_scr[2 * t, r : r + 32, :] = left
            s_scr[2 * t + 1, r : r + 32, :] = right
            newest = jnp.maximum(left, right)
            if t > 0:
                before = max_scr[r : r + 32, :]
                newest = jnp.maximum(newest, before)
            total = jnp.exp(left - newest) + jnp.exp(right - newest)
            if t > 0:
                total = total + sum_scr[r : r + 32, :] * jnp.exp(before - newest)
            max_scr[r : r + 32, :] = newest
            sum_scr[r : r + 32, :] = total

    for t in range(members // 2):
        decode(t)
        score(t)

    highest = max_scr[...]
    row_max = jnp.max(highest, axis=1, keepdims=True)
    total = jnp.sum(sum_scr[...] * jnp.exp(highest - row_max), axis=1, keepdims=True)
    total_scr[...] = jnp.broadcast_to(row_max + jnp.log(total), (queries, LANES))

    def extras(block):
        weight = block[:, 0:1] + block[:, 1:2] + block[:, 2:3]
        return weight, block[:, 3:4], block[:, 4:5]

    extra = group_ref[:, top + books :, :].reshape(queries, LANES).astype(jnp.float32)
    weight, block, place = extras(extra)
    here = me.astype(jnp.float32)
    lane = lax.broadcasted_iota(jnp.int32, (queries, LANES), 1).astype(jnp.float32)
    is_positive = jnp.where((block == here) & (place == lane), 1.0, 0.0)
    coefficient = (
        weight * (jnp.exp(s_scr[me] - total_scr[...]) - is_positive) * scale
    ).astype(jnp.bfloat16)
    pg_scr[...] = lax.dot_general(
        q_scr[...], coefficient, (((0,), (0,)), ((), ())), preferred_element_type=jnp.float32
    )

    own_codes = group_ref[me, top : top + books, :].astype(jnp.float32)
    level = lax.broadcasted_iota(jnp.int32, (levels, LANES), 0).astype(jnp.float32)
    level = level.astype(jnp.bfloat16)
    one = jnp.ones((16, LANES), jnp.bfloat16)
    zero = jnp.zeros((16, LANES), jnp.bfloat16)
    pair_rows = 2 * sub_width
    upper = lax.broadcasted_iota(jnp.int32, (pair_rows, LANES), 0) < sub_width
    ready = []
    for m in range(0, books, 2):
        tables = []
        for h in range(2):
            row = jnp.broadcast_to(own_codes[m + h : m + h + 1, :], (16, LANES)).astype(
                jnp.bfloat16
            )
            tables.append(
                jnp.concatenate(
                    [
                        jnp.where(row == level[16 * j : 16 * j + 16, :], one, zero)
                        for j in range(levels // 16)
                    ],
                    axis=0,
                )
            )
        terms = pg_scr[sub_width * m : sub_width * m + pair_rows, :]
        sums = lax.dot_general(
            jnp.concatenate(
                [jnp.where(upper, terms, 0.0), jnp.where(upper, 0.0, terms)], axis=1
            ).astype(jnp.bfloat16),
            jnp.concatenate(tables, axis=1),
            (((1,), (1,)), ((), ())),
            preferred_element_type=jnp.float32,
        )
        ready.append(sums)
        if m % 4 == 2:
            at = sub_width * (m - 2)
            both = jnp.concatenate(ready, axis=0).astype(jnp.bfloat16)
            for j in range(levels // LANES):
                gb_ref[j, at : at + 2 * pair_rows, :] = both[:, LANES * j : LANES * (j + 1)]
            ready = []

    own = pl.ds(pl.multiple_of(me * rows, rows), rows)
    weight, block, place = extras(group_ref[me, top + books :, :].astype(jnp.float32))
    own_total = total_scr[own, :]
    own_lane = lax.broadcasted_iota(jnp.int32, (rows, LANES), 1).astype(jnp.float32)
    chosen = jnp.zeros((rows, LANES), jnp.float32)
    grad = jnp.zeros((rows, width), jnp.float32)
    for t in range(members // 2):
        parts = []
        for d in (2 * t, 2 * t + 1):
            scores = s_scr[d, own, :]
            hit = (block == float(d)) & (place == own_lane)
            chosen = chosen + jnp.where(hit, scores, 0.0)
            parts.append(
                weight * (jnp.exp(scores - own_total) - jnp.where(hit, 1.0, 0.0)) * scale
            )
        grad = grad + lax.dot_general(
            jnp.concatenate(parts, axis=1).astype(jnp.bfloat16),
            dec_scr[t],
            (((1,), (1,)), ((), ())),
            preferred_element_type=jnp.float32,
        )
    first = grad.astype(jnp.bfloat16).astype(jnp.float32)
    second = (grad - first).astype(jnp.bfloat16).astype(jnp.float32)
    third = grad - first - second
    parts = jnp.concatenate([first, second, third], axis=0).astype(jnp.bfloat16)
    restored = jnp.zeros((3 * rows, width), jnp.float32)
    for j in range(0, width, span):
        restored = restored + lax.dot_general(
            parts[:, j : j + span],
            order_table(width, books, j, span, jnp.float32),
            (((1,), (1,)), ((), ())),
            preferred_element_type=jnp.float32,
        )
    gq_ref[...] = restored[:rows] + restored[rows : 2 * rows] + restored[2 * rows :]
    loss = weight * (own_total - jnp.sum(chosen, axis=1, keepdims=True))
    diagonal = lax.broadcasted_iota(jnp.int32, (rows, LANES), 0).astype(jnp.float32) == own_lane
    loss_ref[...] = jnp.sum(jnp.where(diagonal, loss, 0.0), axis=0, keepdims=True)[:, :rows]


def widen_kernel(sub_width, part_ref, out_ref):
    halves, width, _ = part_ref.shape
    books = width // sub_width
    start = lax.broadcasted_iota(jnp.int32, (books, 1), 0) * sub_width
    column = lax.broadcasted_iota(jnp.int32, (books, width), 1)
    table = jnp.concatenate(
        [jnp.where(column - c == start, 1.0, 0.0) for c in range(sub_width)], axis=0
    ).astype(jnp.bfloat16)
    part = jnp.concatenate([part_ref[j] for j in range(halves)], axis=1)
    out_ref[...] = jnp.dot(table, part, preferred_element_type=jnp.float32)


def spread(block, axis):
    copies = jnp.broadcast_to(block[None], (lax.axis_size(axis),) + block.shape)
    return lax.all_to_all(copies, axis, 0, 0)


def per_device(queries, passage_codes, codebooks, positives, loss_weight):
    rows, width = queries.shape
    books = passage_codes.shape[1]
    sub_width, levels = codebooks.shape[1:]
    members = lax.axis_size("db")
    plane = lax.axis_size(PLANE)
    pack_rows = rows * (width // LANES) + books + rows
    scale = 2.5 / math.sqrt(width)
    pack = pl.pallas_call(
        pack_kernel,
        out_shape=jax.ShapeDtypeStruct((members, pack_rows, LANES), jnp.bfloat16),
        name="pack",
    )(queries, passage_codes.T, loss_weight.reshape(1, rows), positives.reshape(1, rows))
    group = lax.all_to_all(pack, "db", 0, 0)
    me = lax.axis_index("db").astype(jnp.int32).reshape(1, 1)
    loss, grad_queries, book_part = pl.pallas_call(
        functools.partial(main_kernel, scale, books),
        out_shape=(
            jax.ShapeDtypeStruct((1, rows), jnp.float32),
            jax.ShapeDtypeStruct((rows, width), jnp.float32),
            jax.ShapeDtypeStruct((levels // LANES, width, LANES), jnp.bfloat16),
        ),
        in_specs=[pl.BlockSpec(memory_space=pltpu.SMEM)]
        + [pl.BlockSpec(memory_space=pltpu.VMEM)] * 2,
        scratch_shapes=[
            pltpu.VMEM((width, levels), jnp.float32),
            pltpu.VMEM((members * rows, width), jnp.bfloat16),
            pltpu.VMEM((members * rows, width), jnp.bfloat16),
            pltpu.VMEM((members // 2, width, 2 * LANES), jnp.bfloat16),
            pltpu.VMEM((members, members * rows, LANES), jnp.float32),
            pltpu.VMEM((members * rows, LANES), jnp.float32),
            pltpu.VMEM((members * rows, LANES), jnp.float32),
            pltpu.VMEM((members * rows, LANES), jnp.float32),
            pltpu.VMEM((width, LANES), jnp.float32),
        ],
        compiler_params=pltpu.CompilerParams(vmem_limit_bytes=24 * 1024 * 1024),
        name="core",
    )(me, group, codebooks.transpose(1, 0, 2).reshape(width, levels))
    part = lax.all_to_all(book_part.reshape(plane, -1, LANES), PLANE, 0, 0)
    part = jnp.sum(part.astype(jnp.float32), axis=0).astype(jnp.bfloat16)
    part = spread(part, "far")
    part = jnp.sum(part.astype(jnp.float32), axis=0).astype(jnp.bfloat16)
    part = spread(part, PLANE).reshape(-1, width, LANES)
    book_total = pl.pallas_call(
        functools.partial(widen_kernel, sub_width),
        out_shape=jax.ShapeDtypeStruct((width, levels), jnp.float32),
        compiler_params=pltpu.CompilerParams(vmem_limit_bytes=8 * 1024 * 1024),
        name="widen",
    )(part)
    book_total = book_total.reshape(sub_width, books, levels).transpose(1, 0, 2)
    return loss.reshape(rows), grad_queries, book_total


def solution(mesh):
    lines, stacks = mesh.devices.shape
    fine = Mesh(mesh.devices.reshape(lines, 2, stacks // 4, 2), WHOLE)
    return jax.shard_map(
        per_device,
        mesh=fine,
        in_specs=(P(WHOLE, None), P(WHOLE, None), P(), P(WHOLE), P(WHOLE)),
        out_specs=(P(WHOLE), P(WHOLE, None), P()),
        check_vma=False,
    )
```

```python
import functools
import math

import jax
import jax.numpy as jnp
from jax import lax
from jax.experimental import pallas as pl
from jax.experimental.pallas import tpu as pltpu
from jax.sharding import Mesh
from jax.sharding import PartitionSpec as P

LANES = 128
PLANE = ("db", "near", "pair")
WHOLE = ("db", "near", "far", "pair")


def order_table(width, books, start, count, kind):
    sub_width = width // books
    row = lax.broadcasted_iota(jnp.int32, (width, count), 0).astype(kind)
    place = lax.broadcasted_iota(jnp.int32, (1, count), 1) + start
    inner = place % (8 * sub_width)
    source = (place // (8 * sub_width) * 8 + inner % 8) * sub_width + inner // 8
    return jnp.where(row == source.astype(kind), 1.0, 0.0).astype(jnp.bfloat16)


def pack_kernel(queries_ref, codes_ref, weight_ref, positive_ref, out_ref):
    rows, width = queries_ref.shape
    books = codes_ref.shape[0]
    top = rows * (width // LANES)
    code_rows = codes_ref[...].astype(jnp.float32).astype(jnp.bfloat16)
    spot = lax.broadcasted_iota(jnp.int32, (rows, rows), 0)
    lane = lax.broadcasted_iota(jnp.int32, (rows, rows), 1)

    def column(row):
        spread_row = jnp.broadcast_to(row, (rows, rows))
        return jnp.sum(jnp.where(spot == lane, spread_row, 0.0), axis=1, keepdims=True)

    weight = column(weight_ref[...])
    positive = positive_ref[...]
    first = weight.astype(jnp.bfloat16).astype(jnp.float32)
    second = (weight - first).astype(jnp.bfloat16).astype(jnp.float32)
    third = weight - first - second
    block = column((positive // LANES).astype(jnp.float32))
    place = column((positive % LANES).astype(jnp.float32))
    wide = lax.broadcasted_iota(jnp.int32, (rows, LANES), 1)
    extra = jnp.zeros((rows, LANES), jnp.float32)
    for j, value in enumerate((first, second, third, block, place)):
        extra = jnp.where(wide == j, value, extra)
    extra = extra.astype(jnp.bfloat16)
    for d in range(out_ref.shape[0]):
        for j in range(width // LANES):
            out_ref[d, rows * j : rows * (j + 1), :] = queries_ref[
                :, LANES * j : LANES * (j + 1)
            ]
        out_ref[d, top : top + books, :] = code_rows
        out_ref[d, top + books :, :] = extra


def main_kernel(
    scale, books, me_ref, group_ref, cb_ref,
    loss_ref, gq_ref, gb_ref,
    cb_scr, q_scr, sorted_scr, dec_scr, s_scr, max_scr, sum_scr, total_scr, pg_scr,
):
    members = group_ref.shape[0]
    width, levels = cb_ref.shape
    sub_width = width // books
    rows = gq_ref.shape[0]
    blocks = width // LANES
    top = rows * blocks
    queries = members * rows
    me = me_ref[0, 0]
    cb_scr[...] = cb_ref[...].astype(jnp.float32)
    for j in range(blocks):
        q_scr[:, LANES * j : LANES * (j + 1)] = group_ref[
            :, rows * j : rows * (j + 1), :
        ].reshape(queries, LANES)
    span = 2 * LANES
    for j in range(0, width, span):
        sorted_scr[:, j : j + span] = jnp.dot(
            q_scr[...],
            order_table(width, books, j, span, jnp.int32),
            preferred_element_type=jnp.float32,
        ).astype(jnp.bfloat16)
    done = []

    def decode(t):
        for side in range(2):
            codes = (
                group_ref[2 * t + side, top : top + books, :]
                .astype(jnp.float32)
                .astype(jnp.int32)
            )
            for g in range(books // 8):
                index = codes[8 * g : 8 * g + 8, :]
                inner = index & (LANES - 1)
                upper = index >= LANES
                if len(done) >= 5:
                    inner = inner + (done[-5] * 0.0).astype(jnp.int32)
                for two in range(sub_width // 2):
                    tiles = []
                    for c in (2 * two, 2 * two + 1):
                        at = c * books + 8 * g
                        low = jnp.take_along_axis(cb_scr[at : at + 8, :LANES], inner, axis=1)
                        high = jnp.take_along_axis(cb_scr[at : at + 8, LANES:], inner, axis=1)
                        tiles.append(jnp.where(upper, high, low))
                    if two == 0:
                        done.append(tiles[0])
                    at = 8 * sub_width * g + 16 * two
                    dec_scr[t, at : at + 16, LANES * side : LANES * side + LANES] = (
                        jnp.concatenate(tiles, axis=0).astype(jnp.bfloat16)
                    )

    def score(t):
        both = jnp.dot(sorted_scr[...], dec_scr[t], preferred_element_type=jnp.float32)
        for r in range(0, queries, 32):
            left = both[r : r + 32, :LANES] * scale
            right = both[r : r + 32, LANES:] * scale
            s_scr[2 * t, r : r + 32, :] = left
            s_scr[2 * t + 1, r : r + 32, :] = right
            newest = jnp.maximum(left, right)
            if t > 0:
                before = max_scr[r : r + 32, :]
                newest = jnp.maximum(newest, before)
            total = jnp.exp(left - newest) + jnp.exp(right - newest)
            if t > 0:
                total = total + sum_scr[r : r + 32, :] * jnp.exp(before - newest)
            max_scr[r : r + 32, :] = newest
            sum_scr[r : r + 32, :] = total

    for t in range(members // 2):
        decode(t)
        score(t)

    highest = max_scr[...]
    row_max = jnp.max(highest, axis=1, keepdims=True)
    total = jnp.sum(sum_scr[...] * jnp.exp(highest - row_max), axis=1, keepdims=True)
    total_scr[...] = jnp.broadcast_to(row_max + jnp.log(total), (queries, LANES))

    def extras(block):
        weight = block[:, 0:1] + block[:, 1:2] + block[:, 2:3]
        return weight, block[:, 3:4], block[:, 4:5]

    extra = group_ref[:, top + books :, :].reshape(queries, LANES).astype(jnp.float32)
    weight, block, place = extras(extra)
    here = me.astype(jnp.float32)
    lane = lax.broadcasted_iota(jnp.int32, (queries, LANES), 1).astype(jnp.float32)
    is_positive = jnp.where((block == here) & (place == lane), 1.0, 0.0)
    coefficient = (
        weight * (jnp.exp(s_scr[me] - total_scr[...]) - is_positive) * scale
    ).astype(jnp.bfloat16)
    pg_scr[...] = lax.dot_general(
        q_scr[...], coefficient, (((0,), (0,)), ((), ())), preferred_element_type=jnp.float32
    )

    own_codes = group_ref[me, top : top + books, :].astype(jnp.float32)
    level = lax.broadcasted_iota(jnp.int32, (levels, LANES), 0).astype(jnp.float32)
    level = level.astype(jnp.bfloat16)
    one = jnp.ones((16, LANES), jnp.bfloat16)
    zero = jnp.zeros((16, LANES), jnp.bfloat16)
    pair_rows = 2 * sub_width
    upper = lax.broadcasted_iota(jnp.int32, (pair_rows, LANES), 0) < sub_width
    ready = []
    for m in range(0, books, 2):
        tables = []
        for h in range(2):
            row = jnp.broadcast_to(own_codes[m + h : m + h + 1, :], (16, LANES)).astype(
                jnp.bfloat16
            )
            tables.append(
                jnp.concatenate(
                    [
                        jnp.where(row == level[16 * j : 16 * j + 16, :], one, zero)
                        for j in range(levels // 16)
                    ],
                    axis=0,
                )
            )
        terms = pg_scr[sub_width * m : sub_width * m + pair_rows, :]
        sums = lax.dot_general(
            jnp.concatenate(
                [jnp.where(upper, terms, 0.0), jnp.where(upper, 0.0, terms)], axis=1
            ).astype(jnp.bfloat16),
            jnp.concatenate(tables, axis=1),
            (((1,), (1,)), ((), ())),
            preferred_element_type=jnp.float32,
        )
        ready.append(sums)
        if m % 4 == 2:
            at = sub_width * (m - 2)
            both = jnp.concatenate(ready, axis=0).astype(jnp.bfloat16)
            for j in range(levels // LANES):
                gb_ref[j, at : at + 2 * pair_rows, :] = both[:, LANES * j : LANES * (j + 1)]
            ready = []

    own = pl.ds(pl.multiple_of(me * rows, rows), rows)
    weight, block, place = extras(group_ref[me, top + books :, :].astype(jnp.float32))
    own_total = total_scr[own, :]
    own_lane = lax.broadcasted_iota(jnp.int32, (rows, LANES), 1).astype(jnp.float32)
    chosen = jnp.zeros((rows, LANES), jnp.float32)
    grad = jnp.zeros((rows, width), jnp.float32)
    for t in range(members // 2):
        parts = []
        for d in (2 * t, 2 * t + 1):
            scores = s_scr[d, own, :]
            hit = (block == float(d)) & (place == own_lane)
            chosen = chosen + jnp.where(hit, scores, 0.0)
            parts.append(
                weight * (jnp.exp(scores - own_total) - jnp.where(hit, 1.0, 0.0)) * scale
            )
        grad = grad + lax.dot_general(
            jnp.concatenate(parts, axis=1).astype(jnp.bfloat16),
            dec_scr[t],
            (((1,), (1,)), ((), ())),
            preferred_element_type=jnp.float32,
        )
    first = grad.astype(jnp.bfloat16).astype(jnp.float32)
    second = (grad - first).astype(jnp.bfloat16).astype(jnp.float32)
    third = grad - first - second
    parts = jnp.concatenate([first, second, third], axis=0).astype(jnp.bfloat16)
    restored = jnp.zeros((3 * rows, width), jnp.float32)
    for j in range(0, width, span):
        restored = restored + lax.dot_general(
            parts[:, j : j + span],
            order_table(width, books, j, span, jnp.float32),
            (((1,), (1,)), ((), ())),
            preferred_element_type=jnp.float32,
        )
    gq_ref[...] = restored[:rows] + restored[rows : 2 * rows] + restored[2 * rows :]
    loss = weight * (own_total - jnp.sum(chosen, axis=1, keepdims=True))
    diagonal = lax.broadcasted_iota(jnp.int32, (rows, LANES), 0).astype(jnp.float32) == own_lane
    loss_ref[...] = jnp.sum(jnp.where(diagonal, loss, 0.0), axis=0, keepdims=True)[:, :rows]


def widen_kernel(sub_width, part_ref, out_ref):
    halves, width, _ = part_ref.shape
    books = width // sub_width
    start = lax.broadcasted_iota(jnp.int32, (books, 1), 0) * sub_width
    column = lax.broadcasted_iota(jnp.int32, (books, width), 1)
    table = jnp.concatenate(
        [jnp.where(column - c == start, 1.0, 0.0) for c in range(sub_width)], axis=0
    ).astype(jnp.bfloat16)
    part = jnp.concatenate([part_ref[j] for j in range(halves)], axis=1)
    out_ref[...] = jnp.dot(table, part, preferred_element_type=jnp.float32)


def spread(block, axis):
    copies = jnp.broadcast_to(block[None], (lax.axis_size(axis),) + block.shape)
    return lax.all_to_all(copies, axis, 0, 0)


def per_device(queries, passage_codes, codebooks, positives, loss_weight):
    rows, width = queries.shape
    books = passage_codes.shape[1]
    sub_width, levels = codebooks.shape[1:]
    members = lax.axis_size("db")
    plane = lax.axis_size(PLANE)
    pack_rows = rows * (width // LANES) + books + rows
    scale = 2.5 / math.sqrt(width)
    pack = pl.pallas_call(
        pack_kernel,
        out_shape=jax.ShapeDtypeStruct((members, pack_rows, LANES), jnp.bfloat16),
        name="pack",
    )(queries, passage_codes.T, loss_weight.reshape(1, rows), positives.reshape(1, rows))
    group = lax.all_to_all(pack, "db", 0, 0)
    me = lax.axis_index("db").astype(jnp.int32).reshape(1, 1)
    loss, grad_queries, book_part = pl.pallas_call(
        functools.partial(main_kernel, scale, books),
        out_shape=(
            jax.ShapeDtypeStruct((1, rows), jnp.float32),
            jax.ShapeDtypeStruct((rows, width), jnp.float32),
            jax.ShapeDtypeStruct((levels // LANES, width, LANES), jnp.bfloat16),
        ),
        in_specs=[pl.BlockSpec(memory_space=pltpu.SMEM)]
        + [pl.BlockSpec(memory_space=pltpu.VMEM)] * 2,
        scratch_shapes=[
            pltpu.VMEM((width, levels), jnp.float32),
            pltpu.VMEM((members * rows, width), jnp.bfloat16),
            pltpu.VMEM((members * rows, width), jnp.bfloat16),
            pltpu.VMEM((members // 2, width, 2 * LANES), jnp.bfloat16),
            pltpu.VMEM((members, members * rows, LANES), jnp.float32),
            pltpu.VMEM((members * rows, LANES), jnp.float32),
            pltpu.VMEM((members * rows, LANES), jnp.float32),
            pltpu.VMEM((members * rows, LANES), jnp.float32),
            pltpu.VMEM((width, LANES), jnp.float32),
        ],
        compiler_params=pltpu.CompilerParams(vmem_limit_bytes=24 * 1024 * 1024),
        name="core",
    )(me, group, codebooks.transpose(1, 0, 2).reshape(width, levels))
    part = lax.all_to_all(book_part.reshape(plane, -1, LANES), PLANE, 0, 0)
    part = jnp.sum(part.astype(jnp.float32), axis=0).astype(jnp.bfloat16)
    part = spread(part, "far")
    part = jnp.sum(part.astype(jnp.float32), axis=0).astype(jnp.bfloat16)
    part = spread(part, PLANE).reshape(-1, width, LANES)
    book_total = pl.pallas_call(
        functools.partial(widen_kernel, sub_width),
        out_shape=jax.ShapeDtypeStruct((width, levels), jnp.float32),
        compiler_params=pltpu.CompilerParams(vmem_limit_bytes=8 * 1024 * 1024),
        name="widen",
    )(part)
    book_total = book_total.reshape(sub_width, books, levels).transpose(1, 0, 2)
    return loss.reshape(rows), grad_queries, book_total


def solution(mesh):
    lines, stacks = mesh.devices.shape
    fine = Mesh(mesh.devices.reshape(lines, 2, stacks // 4, 2), WHOLE)
    return jax.shard_map(
        per_device,
        mesh=fine,
        in_specs=(P(WHOLE, None), P(WHOLE, None), P(), P(WHOLE), P(WHOLE)),
        out_specs=(P(WHOLE), P(WHOLE, None), P()),
        check_vma=False,
    )
```

```python
import functools
import math

import jax
import jax.numpy as jnp
from jax import lax
from jax.experimental import pallas as pl
from jax.experimental.pallas import tpu as pltpu
from jax.sharding import Mesh
from jax.sharding import PartitionSpec as P

LANES = 128
PLANE = ("db", "near", "pair")
WHOLE = ("db", "near", "far", "pair")


def order_kernel(books, after_ref, table_ref):
    width = table_ref.shape[0]
    sub_width = width // books
    column = lax.broadcasted_iota(jnp.int32, (8, width), 1)
    spot = lax.broadcasted_iota(jnp.int32, (8, width), 0) * sub_width
    for r in range(0, width, 16):
        tiles = []
        for at in (r, r + 8):
            g, c = at // (8 * sub_width), at // 8 % sub_width
            tiles.append(jnp.where(column - (8 * g * sub_width + c) == spot, 1.0, 0.0))
        table_ref[r : r + 16, :] = jnp.concatenate(tiles, axis=0).astype(jnp.bfloat16)


def pack_kernel(queries_ref, codes_ref, weight_ref, positive_ref, out_ref):
    rows, width = queries_ref.shape
    books = codes_ref.shape[0]
    top = rows * (width // LANES)
    code_rows = codes_ref[...].astype(jnp.float32).astype(jnp.bfloat16)
    spot = lax.broadcasted_iota(jnp.int32, (rows, rows), 0)
    lane = lax.broadcasted_iota(jnp.int32, (rows, rows), 1)

    def column(row):
        spread_row = jnp.broadcast_to(row, (rows, rows))
        return jnp.sum(jnp.where(spot == lane, spread_row, 0.0), axis=1, keepdims=True)

    weight = column(weight_ref[...])
    positive = positive_ref[...]
    first = weight.astype(jnp.bfloat16).astype(jnp.float32)
    second = (weight - first).astype(jnp.bfloat16).astype(jnp.float32)
    third = weight - first - second
    block = column((positive // LANES).astype(jnp.float32))
    place = column((positive % LANES).astype(jnp.float32))
    wide = lax.broadcasted_iota(jnp.int32, (rows, LANES), 1)
    extra = jnp.zeros((rows, LANES), jnp.float32)
    for j, value in enumerate((first, second, third, block, place)):
        extra = jnp.where(wide == j, value, extra)
    extra = extra.astype(jnp.bfloat16)
    for d in range(out_ref.shape[0]):
        for j in range(width // LANES):
            out_ref[d, rows * j : rows * (j + 1), :] = queries_ref[
                :, LANES * j : LANES * (j + 1)
            ]
        out_ref[d, top : top + books, :] = code_rows
        out_ref[d, top + books :, :] = extra


def main_kernel(
    scale, books, me_ref, group_ref, cb_ref, table_ref,
    loss_ref, gq_ref, gb_ref,
    cb_scr, q_scr, sorted_scr, dec_scr, s_scr, max_scr, sum_scr, total_scr, pg_scr,
):
    members = group_ref.shape[0]
    width, levels = cb_ref.shape
    sub_width = width // books
    rows = gq_ref.shape[0]
    blocks = width // LANES
    top = rows * blocks
    queries = members * rows
    me = me_ref[0, 0]
    cb_scr[...] = cb_ref[...].astype(jnp.float32)
    for j in range(blocks):
        q_scr[:, LANES * j : LANES * (j + 1)] = group_ref[
            :, rows * j : rows * (j + 1), :
        ].reshape(queries, LANES)
    sorted_scr[...] = lax.dot_general(
        q_scr[...],
        table_ref[...],
        (((1,), (1,)), ((), ())),
        preferred_element_type=jnp.float32,
    ).astype(jnp.bfloat16)

    done = []

    def decode(t):
        for side in range(2):
            codes = (
                group_ref[2 * t + side, top : top + books, :]
                .astype(jnp.float32)
                .astype(jnp.int32)
            )
            for g in range(books // 8):
                index = codes[8 * g : 8 * g + 8, :]
                inner = index & (LANES - 1)
                upper = index >= LANES
                if len(done) >= 5:
                    inner = inner + (done[-5] * 0.0).astype(jnp.int32)
                for two in range(sub_width // 2):
                    tiles = []
                    for c in (2 * two, 2 * two + 1):
                        at = c * books + 8 * g
                        low = jnp.take_along_axis(cb_scr[at : at + 8, :LANES], inner, axis=1)
                        high = jnp.take_along_axis(cb_scr[at : at + 8, LANES:], inner, axis=1)
                        tiles.append(jnp.where(upper, high, low))
                    if two == 0:
                        done.append(tiles[0])
                    at = 8 * sub_width * g + 16 * two
                    dec_scr[t, at : at + 16, LANES * side : LANES * side + LANES] = (
                        jnp.concatenate(tiles, axis=0).astype(jnp.bfloat16)
                    )

    def score(t):
        both = jnp.dot(sorted_scr[...], dec_scr[t], preferred_element_type=jnp.float32)
        for r in range(0, queries, 32):
            left = both[r : r + 32, :LANES] * scale
            right = both[r : r + 32, LANES:] * scale
            s_scr[2 * t, r : r + 32, :] = left
            s_scr[2 * t + 1, r : r + 32, :] = right
            newest = jnp.maximum(left, right)
            if t > 0:
                before = max_scr[r : r + 32, :]
                newest = jnp.maximum(newest, before)
            total = jnp.exp(left - newest) + jnp.exp(right - newest)
            if t > 0:
                total = total + sum_scr[r : r + 32, :] * jnp.exp(before - newest)
            max_scr[r : r + 32, :] = newest
            sum_scr[r : r + 32, :] = total

    for t in range(members // 2):
        decode(t)
        score(t)

    highest = max_scr[...]
    row_max = jnp.max(highest, axis=1, keepdims=True)
    total = jnp.sum(sum_scr[...] * jnp.exp(highest - row_max), axis=1, keepdims=True)
    total_scr[...] = jnp.broadcast_to(row_max + jnp.log(total), (queries, LANES))

    def extras(block):
        weight = block[:, 0:1] + block[:, 1:2] + block[:, 2:3]
        return weight, block[:, 3:4], block[:, 4:5]

    extra = group_ref[:, top + books :, :].reshape(queries, LANES).astype(jnp.float32)
    weight, block, place = extras(extra)
    here = me.astype(jnp.float32)
    lane = lax.broadcasted_iota(jnp.int32, (queries, LANES), 1).astype(jnp.float32)
    is_positive = jnp.where((block == here) & (place == lane), 1.0, 0.0)
    coefficient = (
        weight * (jnp.exp(s_scr[me] - total_scr[...]) - is_positive) * scale
    ).astype(jnp.bfloat16)
    pg_scr[...] = lax.dot_general(
        q_scr[...], coefficient, (((0,), (0,)), ((), ())), preferred_element_type=jnp.float32
    )

    own_codes = group_ref[me, top : top + books, :].astype(jnp.float32)
    level = lax.broadcasted_iota(jnp.int32, (levels, LANES), 0).astype(jnp.float32)
    level = level.astype(jnp.bfloat16)
    one = jnp.ones((16, LANES), jnp.bfloat16)
    zero = jnp.zeros((16, LANES), jnp.bfloat16)
    pair_rows = 2 * sub_width
    upper = lax.broadcasted_iota(jnp.int32, (pair_rows, LANES), 0) < sub_width
    ready = []
    for m in range(0, books, 2):
        tables = []
        for h in range(2):
            row = jnp.broadcast_to(own_codes[m + h : m + h + 1, :], (16, LANES)).astype(
                jnp.bfloat16
            )
            tables.append(
                jnp.concatenate(
                    [
                        jnp.where(row == level[16 * j : 16 * j + 16, :], one, zero)
                        for j in range(levels // 16)
                    ],
                    axis=0,
                )
            )
        terms = pg_scr[sub_width * m : sub_width * m + pair_rows, :]
        sums = lax.dot_general(
            jnp.concatenate(
                [jnp.where(upper, terms, 0.0), jnp.where(upper, 0.0, terms)], axis=1
            ).astype(jnp.bfloat16),
            jnp.concatenate(tables, axis=1),
            (((1,), (1,)), ((), ())),
            preferred_element_type=jnp.float32,
        )
        ready.append(sums)
        if m % 4 == 2:
            at = sub_width * (m - 2)
            both = jnp.concatenate(ready, axis=0).astype(jnp.bfloat16)
            for j in range(levels // LANES):
                gb_ref[j, at : at + 2 * pair_rows, :] = both[:, LANES * j : LANES * (j + 1)]
            ready = []

    own = pl.ds(pl.multiple_of(me * rows, rows), rows)
    weight, block, place = extras(group_ref[me, top + books :, :].astype(jnp.float32))
    own_total = total_scr[own, :]
    own_lane = lax.broadcasted_iota(jnp.int32, (rows, LANES), 1).astype(jnp.float32)
    chosen = jnp.zeros((rows, LANES), jnp.float32)
    grad = jnp.zeros((rows, width), jnp.float32)
    for t in range(members // 2):
        parts = []
        for d in (2 * t, 2 * t + 1):
            scores = s_scr[d, own, :]
            hit = (block == float(d)) & (place == own_lane)
            chosen = chosen + jnp.where(hit, scores, 0.0)
            parts.append(
                weight * (jnp.exp(scores - own_total) - jnp.where(hit, 1.0, 0.0)) * scale
            )
        grad = grad + lax.dot_general(
            jnp.concatenate(parts, axis=1).astype(jnp.bfloat16),
            dec_scr[t],
            (((1,), (1,)), ((), ())),
            preferred_element_type=jnp.float32,
        )
    first = grad.astype(jnp.bfloat16).astype(jnp.float32)
    second = (grad - first).astype(jnp.bfloat16).astype(jnp.float32)
    third = grad - first - second
    restored = jnp.dot(
        jnp.concatenate([first, second, third], axis=0).astype(jnp.bfloat16),
        table_ref[...],
        preferred_element_type=jnp.float32,
    )
    gq_ref[...] = restored[:rows] + restored[rows : 2 * rows] + restored[2 * rows :]
    loss = weight * (own_total - jnp.sum(chosen, axis=1, keepdims=True))
    diagonal = lax.broadcasted_iota(jnp.int32, (rows, LANES), 0).astype(jnp.float32) == own_lane
    loss_ref[...] = jnp.sum(jnp.where(diagonal, loss, 0.0), axis=0, keepdims=True)[:, :rows]


def widen_kernel(sub_width, part_ref, table_ref, out_ref):
    halves, width, _ = part_ref.shape
    books = width // sub_width
    part = jnp.concatenate([part_ref[j] for j in range(halves)], axis=1)
    rows = jnp.dot(table_ref[...], part, preferred_element_type=jnp.float32)
    for g in range(books // 8):
        for c in range(sub_width):
            at = 8 * (g * sub_width + c)
            out_ref[c * books + 8 * g : c * books + 8 * g + 8, :] = rows[at : at + 8, :]


def spread(block, axis):
    copies = jnp.broadcast_to(block[None], (lax.axis_size(axis),) + block.shape)
    return lax.all_to_all(copies, axis, 0, 0)


def per_device(queries, passage_codes, codebooks, positives, loss_weight):
    rows, width = queries.shape
    books = passage_codes.shape[1]
    sub_width, levels = codebooks.shape[1:]
    members = lax.axis_size("db")
    plane = lax.axis_size(PLANE)
    pack_rows = rows * (width // LANES) + books + rows
    scale = 2.5 / math.sqrt(width)
    pack = pl.pallas_call(
        pack_kernel,
        out_shape=jax.ShapeDtypeStruct((members, pack_rows, LANES), jnp.bfloat16),
        name="pack",
    )(queries, passage_codes.T, loss_weight.reshape(1, rows), positives.reshape(1, rows))
    group = lax.all_to_all(pack, "db", 0, 0)
    table = pl.pallas_call(
        functools.partial(order_kernel, books),
        out_shape=jax.ShapeDtypeStruct((width, width), jnp.bfloat16),
        in_specs=[pl.BlockSpec(memory_space=pl.ANY)],
        compiler_params=pltpu.CompilerParams(vmem_limit_bytes=8 * 1024 * 1024),
        cost_estimate=pl.CostEstimate(
            flops=width * width, bytes_accessed=2 * width * width, transcendentals=0
        ),
        name="order",
    )(pack)
    me = lax.axis_index("db").astype(jnp.int32).reshape(1, 1)
    loss, grad_queries, book_part = pl.pallas_call(
        functools.partial(main_kernel, scale, books),
        out_shape=(
            jax.ShapeDtypeStruct((1, rows), jnp.float32),
            jax.ShapeDtypeStruct((rows, width), jnp.float32),
            jax.ShapeDtypeStruct((levels // LANES, width, LANES), jnp.bfloat16),
        ),
        in_specs=[pl.BlockSpec(memory_space=pltpu.SMEM)]
        + [pl.BlockSpec(memory_space=pltpu.VMEM)] * 3,
        scratch_shapes=[
            pltpu.VMEM((width, levels), jnp.float32),
            pltpu.VMEM((members * rows, width), jnp.bfloat16),
            pltpu.VMEM((members * rows, width), jnp.bfloat16),
            pltpu.VMEM((members // 2, width, 2 * LANES), jnp.bfloat16),
            pltpu.VMEM((members, members * rows, LANES), jnp.float32),
            pltpu.VMEM((members * rows, LANES), jnp.float32),
            pltpu.VMEM((members * rows, LANES), jnp.float32),
            pltpu.VMEM((members * rows, LANES), jnp.float32),
            pltpu.VMEM((width, LANES), jnp.float32),
        ],
        compiler_params=pltpu.CompilerParams(vmem_limit_bytes=24 * 1024 * 1024),
        name="core",
    )(me, group, codebooks.transpose(1, 0, 2).reshape(width, levels), table)
    part = lax.all_to_all(book_part.reshape(plane, -1, LANES), PLANE, 0, 0)
    part = jnp.sum(part.astype(jnp.float32), axis=0).astype(jnp.bfloat16)
    part = spread(part, "far")
    part = jnp.sum(part.astype(jnp.float32), axis=0).astype(jnp.bfloat16)
    part = spread(part, PLANE).reshape(-1, width, LANES)
    book_total = pl.pallas_call(
        functools.partial(widen_kernel, sub_width),
        out_shape=jax.ShapeDtypeStruct((width, levels), jnp.float32),
        compiler_params=pltpu.CompilerParams(vmem_limit_bytes=8 * 1024 * 1024),
        name="widen",
    )(part, table)
    book_total = book_total.reshape(sub_width, books, levels).transpose(1, 0, 2)
    return loss.reshape(rows), grad_queries, book_total


def solution(mesh):
    lines, stacks = mesh.devices.shape
    fine = Mesh(mesh.devices.reshape(lines, 2, stacks // 4, 2), WHOLE)
    return jax.shard_map(
        per_device,
        mesh=fine,
        in_specs=(P(WHOLE, None), P(WHOLE, None), P(), P(WHOLE), P(WHOLE)),
        out_specs=(P(WHOLE), P(WHOLE, None), P()),
        check_vma=False,
    )
```

```python
import functools
import math

import jax
import jax.numpy as jnp
from jax import lax
from jax.experimental import pallas as pl
from jax.experimental.pallas import tpu as pltpu
from jax.sharding import Mesh
from jax.sharding import PartitionSpec as P

LANES = 128
PLANE = ("db", "near", "pair")
WHOLE = ("db", "near", "far", "pair")


def order_kernel(books, after_ref, table_ref):
    width = table_ref.shape[0]
    sub_width = width // books
    column = lax.broadcasted_iota(jnp.int32, (8, width), 1)
    spot = lax.broadcasted_iota(jnp.int32, (8, width), 0) * sub_width
    for r in range(0, width, 16):
        tiles = []
        for at in (r, r + 8):
            g, c = at // (8 * sub_width), at // 8 % sub_width
            tiles.append(jnp.where(column - (8 * g * sub_width + c) == spot, 1.0, 0.0))
        table_ref[r : r + 16, :] = jnp.concatenate(tiles, axis=0).astype(jnp.bfloat16)


def pack_kernel(queries_ref, codes_ref, weight_ref, positive_ref, out_ref):
    rows, width = queries_ref.shape
    books = codes_ref.shape[0]
    top = rows * (width // LANES)
    code_rows = codes_ref[...].astype(jnp.float32).astype(jnp.bfloat16)
    spot = lax.broadcasted_iota(jnp.int32, (rows, rows), 0)
    lane = lax.broadcasted_iota(jnp.int32, (rows, rows), 1)

    def column(row):
        spread_row = jnp.broadcast_to(row, (rows, rows))
        return jnp.sum(jnp.where(spot == lane, spread_row, 0.0), axis=1, keepdims=True)

    weight = column(weight_ref[...])
    positive = positive_ref[...]
    first = weight.astype(jnp.bfloat16).astype(jnp.float32)
    second = (weight - first).astype(jnp.bfloat16).astype(jnp.float32)
    third = weight - first - second
    block = column((positive // LANES).astype(jnp.float32))
    place = column((positive % LANES).astype(jnp.float32))
    wide = lax.broadcasted_iota(jnp.int32, (rows, LANES), 1)
    extra = jnp.zeros((rows, LANES), jnp.float32)
    for j, value in enumerate((first, second, third, block, place)):
        extra = jnp.where(wide == j, value, extra)
    extra = extra.astype(jnp.bfloat16)
    for d in range(out_ref.shape[0]):
        for j in range(width // LANES):
            out_ref[d, rows * j : rows * (j + 1), :] = queries_ref[
                :, LANES * j : LANES * (j + 1)
            ]
        out_ref[d, top : top + books, :] = code_rows
        out_ref[d, top + books :, :] = extra


def main_kernel(
    scale, books, me_ref, group_ref, cb_ref, table_ref,
    loss_ref, gq_ref, gb_ref,
    cb_scr, q_scr, sorted_scr, dec_scr, s_scr, max_scr, sum_scr, total_scr, pg_scr,
):
    members = group_ref.shape[0]
    width, levels = cb_ref.shape
    sub_width = width // books
    rows = gq_ref.shape[0]
    blocks = width // LANES
    top = rows * blocks
    queries = members * rows
    me = me_ref[0, 0]
    cb_scr[...] = cb_ref[...].astype(jnp.float32)
    for j in range(blocks):
        q_scr[:, LANES * j : LANES * (j + 1)] = group_ref[
            :, rows * j : rows * (j + 1), :
        ].reshape(queries, LANES)
    sorted_scr[...] = lax.dot_general(
        q_scr[...],
        table_ref[...],
        (((1,), (1,)), ((), ())),
        preferred_element_type=jnp.float32,
    ).astype(jnp.bfloat16)

    done = []

    def decode(t):
        for side in range(2):
            codes = (
                group_ref[2 * t + side, top : top + books, :]
                .astype(jnp.float32)
                .astype(jnp.int32)
            )
            for g in range(books // 8):
                index = codes[8 * g : 8 * g + 8, :]
                inner = index & (LANES - 1)
                upper = index >= LANES
                if len(done) >= 5:
                    inner = inner + (done[-5] * 0.0).astype(jnp.int32)
                for two in range(sub_width // 2):
                    tiles = []
                    for c in (2 * two, 2 * two + 1):
                        at = c * books + 8 * g
                        low = jnp.take_along_axis(cb_scr[at : at + 8, :LANES], inner, axis=1)
                        high = jnp.take_along_axis(cb_scr[at : at + 8, LANES:], inner, axis=1)
                        tiles.append(jnp.where(upper, high, low))
                    if two == 0:
                        done.append(tiles[0])
                    at = 8 * sub_width * g + 16 * two
                    dec_scr[t, at : at + 16, LANES * side : LANES * side + LANES] = (
                        jnp.concatenate(tiles, axis=0).astype(jnp.bfloat16)
                    )

    def score(t):
        both = jnp.dot(sorted_scr[...], dec_scr[t], preferred_element_type=jnp.float32)
        for r in range(0, queries, 32):
            left = both[r : r + 32, :LANES] * scale
            right = both[r : r + 32, LANES:] * scale
            s_scr[2 * t, r : r + 32, :] = left
            s_scr[2 * t + 1, r : r + 32, :] = right
            newest = jnp.maximum(left, right)
            if t > 0:
                before = max_scr[r : r + 32, :]
                newest = jnp.maximum(newest, before)
            total = jnp.exp(left - newest) + jnp.exp(right - newest)
            if t > 0:
                total = total + sum_scr[r : r + 32, :] * jnp.exp(before - newest)
            max_scr[r : r + 32, :] = newest
            sum_scr[r : r + 32, :] = total

    for t in range(members // 2):
        decode(t)
        score(t)

    highest = max_scr[...]
    row_max = jnp.max(highest, axis=1, keepdims=True)
    total = jnp.sum(sum_scr[...] * jnp.exp(highest - row_max), axis=1, keepdims=True)
    total_scr[...] = jnp.broadcast_to(row_max + jnp.log(total), (queries, LANES))

    def extras(block):
        weight = block[:, 0:1] + block[:, 1:2] + block[:, 2:3]
        return weight, block[:, 3:4], block[:, 4:5]

    extra = group_ref[:, top + books :, :].reshape(queries, LANES).astype(jnp.float32)
    weight, block, place = extras(extra)
    here = me.astype(jnp.float32)
    lane = lax.broadcasted_iota(jnp.int32, (queries, LANES), 1).astype(jnp.float32)
    is_positive = jnp.where((block == here) & (place == lane), 1.0, 0.0)
    coefficient = (
        weight * (jnp.exp(s_scr[me] - total_scr[...]) - is_positive) * scale
    ).astype(jnp.bfloat16)
    pg_scr[...] = lax.dot_general(
        q_scr[...], coefficient, (((0,), (0,)), ((), ())), preferred_element_type=jnp.float32
    )

    own_codes = group_ref[me, top : top + books, :].astype(jnp.float32)
    level = lax.broadcasted_iota(jnp.int32, (levels, LANES), 0).astype(jnp.float32)
    level = level.astype(jnp.bfloat16)
    one = jnp.ones((16, LANES), jnp.bfloat16)
    zero = jnp.zeros((16, LANES), jnp.bfloat16)
    pair_rows = 2 * sub_width
    upper = lax.broadcasted_iota(jnp.int32, (pair_rows, LANES), 0) < sub_width
    ready = []
    for m in range(0, books, 2):
        tables = []
        for h in range(2):
            row = jnp.broadcast_to(own_codes[m + h : m + h + 1, :], (16, LANES)).astype(
                jnp.bfloat16
            )
            tables.append(
                jnp.concatenate(
                    [
                        jnp.where(row == level[16 * j : 16 * j + 16, :], one, zero)
                        for j in range(levels // 16)
                    ],
                    axis=0,
                )
            )
        terms = pg_scr[sub_width * m : sub_width * m + pair_rows, :]
        sums = lax.dot_general(
            jnp.concatenate(
                [jnp.where(upper, terms, 0.0), jnp.where(upper, 0.0, terms)], axis=1
            ).astype(jnp.bfloat16),
            jnp.concatenate(tables, axis=1),
            (((1,), (1,)), ((), ())),
            preferred_element_type=jnp.float32,
        )
        ready.append(sums)
        if m % 4 == 2:
            at = sub_width * (m - 2)
            both = jnp.concatenate(ready, axis=0).astype(jnp.bfloat16)
            for j in range(levels // LANES):
                gb_ref[j, at : at + 2 * pair_rows, :] = both[:, LANES * j : LANES * (j + 1)]
            ready = []

    own = pl.ds(pl.multiple_of(me * rows, rows), rows)
    weight, block, place = extras(group_ref[me, top + books :, :].astype(jnp.float32))
    own_total = total_scr[own, :]
    own_lane = lax.broadcasted_iota(jnp.int32, (rows, LANES), 1).astype(jnp.float32)
    chosen = jnp.zeros((rows, LANES), jnp.float32)
    grad = jnp.zeros((rows, width), jnp.float32)
    for t in range(members // 2):
        parts = []
        for d in (2 * t, 2 * t + 1):
            scores = s_scr[d, own, :]
            hit = (block == float(d)) & (place == own_lane)
            chosen = chosen + jnp.where(hit, scores, 0.0)
            parts.append(
                weight * (jnp.exp(scores - own_total) - jnp.where(hit, 1.0, 0.0)) * scale
            )
        grad = grad + lax.dot_general(
            jnp.concatenate(parts, axis=1).astype(jnp.bfloat16),
            dec_scr[t],
            (((1,), (1,)), ((), ())),
            preferred_element_type=jnp.float32,
        )
    first = grad.astype(jnp.bfloat16).astype(jnp.float32)
    second = (grad - first).astype(jnp.bfloat16).astype(jnp.float32)
    third = grad - first - second
    restored = jnp.dot(
        jnp.concatenate([first, second, third], axis=0).astype(jnp.bfloat16),
        table_ref[...],
        preferred_element_type=jnp.float32,
    )
    gq_ref[...] = restored[:rows] + restored[rows : 2 * rows] + restored[2 * rows :]
    loss = weight * (own_total - jnp.sum(chosen, axis=1, keepdims=True))
    diagonal = lax.broadcasted_iota(jnp.int32, (rows, LANES), 0).astype(jnp.float32) == own_lane
    loss_ref[...] = jnp.sum(jnp.where(diagonal, loss, 0.0), axis=0, keepdims=True)[:, :rows]


def widen_kernel(sub_width, part_ref, table_ref, out_ref):
    halves, width, _ = part_ref.shape
    books = width // sub_width
    span = 8 * sub_width
    block = table_ref[:span, :span]
    for g in range(books // 8):
        part = jnp.concatenate(
            [part_ref[j, span * g : span * (g + 1), :] for j in range(halves)], axis=1
        )
        rows = jnp.dot(block, part, preferred_element_type=jnp.float32)
        for c in range(sub_width):
            out_ref[c * books + 8 * g : c * books + 8 * g + 8, :] = rows[8 * c : 8 * c + 8, :]


def spread(block, axis):
    copies = jnp.broadcast_to(block[None], (lax.axis_size(axis),) + block.shape)
    return lax.all_to_all(copies, axis, 0, 0)


def per_device(queries, passage_codes, codebooks, positives, loss_weight):
    rows, width = queries.shape
    books = passage_codes.shape[1]
    sub_width, levels = codebooks.shape[1:]
    members = lax.axis_size("db")
    plane = lax.axis_size(PLANE)
    pack_rows = rows * (width // LANES) + books + rows
    scale = 2.5 / math.sqrt(width)
    pack = pl.pallas_call(
        pack_kernel,
        out_shape=jax.ShapeDtypeStruct((members, pack_rows, LANES), jnp.bfloat16),
        name="pack",
    )(queries, passage_codes.T, loss_weight.reshape(1, rows), positives.reshape(1, rows))
    group = lax.all_to_all(pack, "db", 0, 0)
    table = pl.pallas_call(
        functools.partial(order_kernel, books),
        out_shape=jax.ShapeDtypeStruct((width, width), jnp.bfloat16),
        in_specs=[pl.BlockSpec(memory_space=pl.ANY)],
        compiler_params=pltpu.CompilerParams(vmem_limit_bytes=8 * 1024 * 1024),
        cost_estimate=pl.CostEstimate(
            flops=width * width, bytes_accessed=2 * width * width, transcendentals=0
        ),
        name="order",
    )(pack)
    me = lax.axis_index("db").astype(jnp.int32).reshape(1, 1)
    loss, grad_queries, book_part = pl.pallas_call(
        functools.partial(main_kernel, scale, books),
        out_shape=(
            jax.ShapeDtypeStruct((1, rows), jnp.float32),
            jax.ShapeDtypeStruct((rows, width), jnp.float32),
            jax.ShapeDtypeStruct((levels // LANES, width, LANES), jnp.bfloat16),
        ),
        in_specs=[pl.BlockSpec(memory_space=pltpu.SMEM)]
        + [pl.BlockSpec(memory_space=pltpu.VMEM)] * 3,
        scratch_shapes=[
            pltpu.VMEM((width, levels), jnp.float32),
            pltpu.VMEM((members * rows, width), jnp.bfloat16),
            pltpu.VMEM((members * rows, width), jnp.bfloat16),
            pltpu.VMEM((members // 2, width, 2 * LANES), jnp.bfloat16),
            pltpu.VMEM((members, members * rows, LANES), jnp.float32),
            pltpu.VMEM((members * rows, LANES), jnp.float32),
            pltpu.VMEM((members * rows, LANES), jnp.float32),
            pltpu.VMEM((members * rows, LANES), jnp.float32),
            pltpu.VMEM((width, LANES), jnp.float32),
        ],
        compiler_params=pltpu.CompilerParams(vmem_limit_bytes=24 * 1024 * 1024),
        name="core",
    )(me, group, codebooks.transpose(1, 0, 2).reshape(width, levels), table)
    part = lax.all_to_all(book_part.reshape(plane, -1, LANES), PLANE, 0, 0)
    part = jnp.sum(part.astype(jnp.float32), axis=0).astype(jnp.bfloat16)
    part = spread(part, "far")
    part = jnp.sum(part.astype(jnp.float32), axis=0).astype(jnp.bfloat16)
    part = spread(part, PLANE).reshape(-1, width, LANES)
    book_total = pl.pallas_call(
        functools.partial(widen_kernel, sub_width),
        out_shape=jax.ShapeDtypeStruct((width, levels), jnp.float32),
        compiler_params=pltpu.CompilerParams(vmem_limit_bytes=8 * 1024 * 1024),
        name="widen",
    )(part, table)
    book_total = book_total.reshape(sub_width, books, levels).transpose(1, 0, 2)
    return loss.reshape(rows), grad_queries, book_total


def solution(mesh):
    lines, stacks = mesh.devices.shape
    fine = Mesh(mesh.devices.reshape(lines, 2, stacks // 4, 2), WHOLE)
    return jax.shard_map(
        per_device,
        mesh=fine,
        in_specs=(P(WHOLE, None), P(WHOLE, None), P(), P(WHOLE), P(WHOLE)),
        out_specs=(P(WHOLE), P(WHOLE, None), P()),
        check_vma=False,
    )
```
